32 devices in a mesh: ens: 2 (over y), walk: 8 (over z, x), chol: 2 (over core).
Axes of the slice: x: 2, y: 2, z: 4, core: 2. Of those that a mesh axis runs over, the one named last changes fastest.
Arguments:
- green: bfloat16 [64, 144000], P(('ens', 'walk', 'chol')), parts along dimension 0, may hold values from -6 to 6
- chol_vecs: bfloat16 [8, 144000], P('chol'), may hold values from -0.125 to 0.125
- one_body: bfloat16 [144000], replicated, may hold values from -0.015625 to 0.015625
- weights: float32 [64], P(('ens', 'walk', 'chol')), parts along dimension 0, may hold values from 0.25 to 4
- counts: int32 [32], P(('ens', 'walk', 'chol')), parts along dimension 0, may hold values from 1 to 2, as said below
- copy_list: int32 [64], P('ens'), parts along dimension 0, may hold values from 0 to 31, as said below
- e_median: float32 [2], P('ens'), parts along dimension 0, may hold values from -1 to 1
- clip_bin: int32 [2], P('ens'), parts along dimension 0, may hold values from 128 to 1023
Outputs:
- energy: float32 [64], P(('ens', 'walk', 'chol')), parts along dimension 0
- estimate: float32 [2], P('ens'), parts along dimension 0
- new_weights: float32 [64], P(('ens', 'walk', 'chol')), parts along dimension 0
- new_panels: bfloat16 [64, 144000], P(('ens', 'walk', 'chol')), parts along dimension 0
The draws below stay inside these ranges and needn't reach their ends.
There are 2 independent parts, one for each index of `ens`. The reference program is written for one: setup_inputs(seed, part) draws one part's arguments, and reference() takes and returns one part's arrays. A program takes and returns all parts, laid end to end along the dimension named above; an argument that names none is the same for every part. Nothing has to cross between parts.
Inputs may be any that keep to these rules, and one draw needn't show every extreme that they name: Device h holds walkers h * 2 to h * 2 + 1; the first counts[h] of them are live. `copy_list`: entries never decrease along the slots and name only live walkers.
All inputs are finite; a program needn't handle non-finite values.
Results may differ from the reference program's by a relative error of at most 0.001.
Values may be sent and summed in bfloat16 or wider, within the bound.
A program may use at most 64 MiB of HBM per device.

```python
import math
import jax
import jax.numpy as jnp
from jax import lax

ORB = 1200
ELEC = 120
WALK_DEV = 2
NCHOL = 8
HOLDERS = 16
WALKERS = 32
N_CHOL = 2


def comb_tables(key):
    drawn = jax.random.randint(jax.random.fold_in(key, 11), (HOLDERS,), 1, WALK_DEV + 1)
    places = jnp.arange(HOLDERS)
    counts = jnp.where(places == 0, 1, jnp.where(places == HOLDERS - 1, WALK_DEV, drawn)).astype(jnp.int32)
    walker_ids = jnp.arange(WALKERS)
    alive = walker_ids % WALK_DEV < counts[walker_ids // WALK_DEV]
    tickets = jax.random.randint(jax.random.fold_in(key, 12), (WALKERS,), 1, 9)
    tickets = jnp.where(walker_ids == WALKERS - 1, 16, tickets) * alive.astype(jnp.int32)
    heavy_holder = jax.random.randint(jax.random.fold_in(key, 14), (), 0, HOLDERS)
    tickets = jnp.where(walker_ids == heavy_holder * WALK_DEV, 4 * WALKERS, tickets)
    running = jnp.cumsum(tickets)
    weight_total = running[-1]
    phase_shift = jax.random.randint(jax.random.fold_in(key, 13), (), 0, jnp.minimum(weight_total, WALKERS))
    points = (walker_ids * weight_total + phase_shift) // WALKERS
    sources = jnp.searchsorted(running, points, side='right').astype(jnp.int32)
    return (counts, sources)


def draw_counts(key, part):
    return comb_tables(key)[0]


def draw_copy_list(key, part):
    return comb_tables(key)[1]


def shard_levels(stream_key, extent, shards, smallest, top_value):
    def one(axis_at, shards_of):
        steps = jax.random.uniform(jax.random.fold_in(jax.random.fold_in(stream_key, 6), axis_at), (shards_of,), jnp.float32, smallest / len(shards), top_value / len(shards))
        return jnp.repeat(jnp.exp(steps), extent[axis_at] // shards_of).reshape((-1,) + (1,) * (len(extent) - axis_at - 1))

    gain = one(*shards[0])
    for cut in shards[1:]:
        gain = gain * one(*cut)
    return gain


def noise(key, extent, spread, most, split=(), kind=jnp.bfloat16):
    result = jax.random.normal(key, extent, jnp.float32) * spread
    if len(split) > 0:
        result = shard_levels(key, extent, split, -0.22, 0.18) * result
    return jnp.clip(result, min=-most, max=most).astype(kind)


def setup_inputs(seed: int = 0, part: int = 0) -> dict:
    key_list = jax.random.split(jax.random.key(seed), 9)
    part_splits = jax.random.split(jax.random.fold_in(key_list[8], part), 9)
    return {
        "green": noise(part_splits[0], (WALKERS, ORB * ELEC), 1.0, 6.0, ((0, 16),)),
        "chol_vecs": noise(key_list[1], (NCHOL, ELEC * ORB), (2 * ORB) ** -0.5, 0.125, ((0, 2),)),
        "one_body": noise(key_list[2], (ORB * ELEC,), (ORB * ELEC) ** -0.5, 0.015625),
        "weights": jnp.clip(jnp.exp(math.log(4.0) - 2.7725887 * jax.random.uniform(part_splits[3], (WALKERS,), jnp.float32) ** shard_levels(part_splits[3], (WALKERS,), ((0, 16),), -0.2, 0.2)), 0.25, 4.0),
        "counts": draw_counts(jax.random.fold_in(jax.random.fold_in(key_list[8], part), 71), part),
        "copy_list": draw_copy_list(jax.random.fold_in(jax.random.fold_in(key_list[8], part), 71), part),
        "e_median": jnp.clip(jax.random.uniform(part_splits[6], (1,), jnp.float32, -1.0, 1.0), -1.0, 1.0),
        "clip_bin": jax.random.randint(part_splits[7], (1,), 128, 1024).astype(jnp.int32),
    }


tau_step = 0.2


def slab_terms(block, chol_mat):
    panels = block.astype(jnp.float32).reshape(block.shape[0], ORB, ELEC)
    products = jnp.einsum("gan,wnb->wgab", chol_mat, panels)
    traces = jnp.trace(products, axis1=2, axis2=3)
    coulomb = 0.5 * jnp.sum(traces * traces, axis=1)
    exchange = -0.5 * jnp.sum(products * jnp.swapaxes(products, 2, 3), axis=(1, 2, 3))
    return coulomb + exchange


def reference(green, chol_vecs, one_body, weights, counts, copy_list, e_median, clip_bin):
    chol_mat = chol_vecs.astype(jnp.float32).reshape(NCHOL, ELEC, ORB)
    blocks = green.reshape(WALKERS // (WALK_DEV * N_CHOL), WALK_DEV * N_CHOL, ORB * ELEC)
    two_body = lax.map(lambda block: slab_terms(block, chol_mat), blocks).reshape(WALKERS)
    one_part = jnp.dot(green, one_body, preferred_element_type=jnp.float32)
    energy = one_part + two_body / ELEC
    half_width = clip_bin[0].astype(jnp.float32) / 256.0
    median = e_median[0]
    clipped = jnp.clip(energy, median - half_width, median + half_width)
    walker_ids = jnp.arange(WALKERS, dtype=jnp.int32)
    alive = (walker_ids % WALK_DEV) < counts[walker_ids // WALK_DEV]
    grown_weight = jnp.where(alive, weights * jnp.exp(-tau_step * (clipped - median)), jnp.float32(0.0))
    weight_sum = jnp.sum(grown_weight)
    estimate = (jnp.sum(grown_weight * clipped) / weight_sum).reshape(1)
    new_weights = jnp.take(grown_weight, copy_list) * (WALKERS / weight_sum)
    new_panels = jnp.take(green, copy_list, axis=0)
    return energy, estimate, new_weights, new_panels
```

```python
import functools

import jax
import jax.numpy as jnp
from jax import lax
from jax.experimental import pallas as pl
from jax.experimental.pallas import tpu as pltpu
from jax.sharding import PartitionSpec as P

ORB = 1200
ELEC = 120
LANES = 128
INNER = 6
OUTER = 2
ROW = 2
ROOM = 8


tau_step = 0.2


def layout(n, groups, tiles):
    units = n // 4 * (INNER + OUTER)
    return units, -(-tiles // units)


def body(
    n, groups, unit, room,
    copy_hbm, weight_hbm, median_hbm, count_hbm, clip_hbm,
    panel_ref, chol_hbm, one_hbm,
    landed, energy_hbm, estimate_hbm, fresh_hbm, flag_hbm,
    padded, slab, other, messages,
    panel_rows, theta_rows, theta, slab_rows, products, one_rows,
    chol_ref, one_ref, copy_ref, weight_ref, median_ref, count_ref, clip_ref,
    table, asked, counted, told, energy_ref, estimate_ref, fresh_ref, flag_ref,
    local, sv, rv, out, s1, r1, s2, r2, s3, r3, sc, rc, sw, rw,
    *buffers,
):
    slots, length = panel_ref.shape
    nchol = chol_ref.shape[0]
    half, quarter = n // 2, n // 4
    width = unit * LANES
    line = ROW * groups
    lines = half // line
    spread = buffers[:INNER]
    cross = buffers[INNER : 2 * INNER]
    leaving = buffers[2 * INNER : 3 * INNER]
    picked = buffers[3 * INNER :]
    everything = room >= half * slots
    chol_index = lax.axis_index("chol")
    me = lax.axis_index("walk") * groups + chol_index
    side, here = me // half, me % half
    parts, part = lax.axis_size("ens"), lax.axis_index("ens")
    mesh_ids = pl.DeviceIdType.MESH
    f32, bf16 = jnp.float32, jnp.bfloat16

    def at(j):
        return {"walk": j // groups, "chol": j % groups}

    def flip(j, s):
        r = j // line
        return ((1 - s) * (lines - 1 - r) + s * r) * line + j % line

    mine = flip(here, side)
    inner = mine < quarter

    def start_of(h, k):
        near = h * INNER + k
        far = quarter * INNER + (h - quarter) * OUTER + k
        return pl.multiple_of(jnp.where(h < quarter, near, far) * width, LANES)

    barrier = pltpu.get_barrier_semaphore()
    fetch = pltpu.make_async_copy(
        panel_ref, padded.at[:, pl.ds(0, length)], local.at[0]
    )
    fetch.start()

    def greet(d, c):
        pl.semaphore_signal(
            barrier, inc=1, device_id=at((me + d) % n), device_id_type=mesh_ids
        )
        return c

    lax.fori_loop(1, n, greet, 0)
    for o in range(1, parts):
        pl.semaphore_signal(
            barrier, inc=1, device_id={"ens": (part + o) % parts}, device_id_type=mesh_ids
        )
    fetches = [
        pltpu.make_async_copy(source, target, local.at[1 + i])
        for i, (source, target) in enumerate((
            (chol_hbm, chol_ref), (one_hbm, one_ref), (copy_hbm, copy_ref),
            (weight_hbm, weight_ref), (median_hbm, median_ref),
            (count_hbm, count_ref), (clip_hbm, clip_ref),
        ))
    ]
    for copy in fetches:
        copy.start()
    padded[:, length:] = jnp.zeros((slots, padded.shape[1] - length), bf16)
    fetch.wait()
    pl.semaphore_wait(barrier, n - 1 + parts - 1)

    for k in range(INNER):
        targets = half if k < OUTER else quarter

        def send_slice(d, c):
            h = (mine + d) % targets

            @pl.when(h != mine)
            def _():
                pltpu.make_async_remote_copy(
                    src_ref=padded.at[:, pl.ds(start_of(h, k), width)],
                    dst_ref=spread[k].at[here],
                    send_sem=s1.at[k], recv_sem=r1.at[k],
                    device_id=at(side * half + flip(h, side)), device_id_type=mesh_ids,
                ).start()

            return c

        lax.fori_loop(0, targets, send_slice, 0)
    for k in range(INNER):

        def keep():
            spread[k][here] = padded[:, pl.ds(start_of(mine, k), width)]

        if k < OUTER:
            keep()
        else:
            pl.when(inner)(keep)
    for copy in fetches:
        copy.wait()

    split = half * slots
    base, away = side * split, (1 - side) * split

    def read_own(d, carry):
        before, rank = carry
        source = copy_ref[base + d]
        comes = source // split != side
        fresh = comes & (source != before)
        rank = rank + fresh.astype(jnp.int32)
        place = source - away if everything else jnp.minimum(rank - 1, room - 1)
        table[d] = jnp.where(comes, split + place, source - base)
        return source, rank

    arriving = lax.fori_loop(0, split, read_own, (jnp.int32(-1), jnp.int32(0)))[1]
    votes = []
    if not everything:

        def read_away(d, carry):
            before, rank, chosen = carry
            source = copy_ref[away + d]
            fresh = (source // split == side) & (source != before)
            chosen = tuple(
                jnp.where(fresh & (rank == m), source - base, chosen[m])
                for m in range(room)
            )
            return source, rank + fresh.astype(jnp.int32), chosen

        _, departing, chosen = lax.fori_loop(
            0, split, read_away,
            (jnp.int32(-1), jnp.int32(0), (jnp.int32(0),) * room),
        )
        for m in range(room):
            asked[m] = chosen[m]
        counted[...] = jnp.full(counted.shape, jnp.maximum(arriving, departing), jnp.int32)
        for o in range(1, parts):
            vote = pltpu.make_async_remote_copy(
                src_ref=counted, dst_ref=told.at[o - 1],
                send_sem=sv.at[o - 1], recv_sem=rv.at[o - 1],
                device_id={"ens": (part + o) % parts}, device_id_type=mesh_ids,
            )
            vote.start()
            votes.append(vote)

    step = 8 * LANES
    pieces = [(f, min(step, width - f)) for f in range(0, width, step)]

    def merge(lines_of, size):
        spot = lax.broadcasted_iota(jnp.int32, (slots, size), 0)
        value = None
        for k, (x, row) in enumerate(lines_of):
            picked_line = x[0:1]
            for w in range(1, slots):
                picked_line = jnp.where(row == w, x[w : w + 1], picked_line)
            picked_line = jnp.broadcast_to(picked_line, (slots, size))
            value = picked_line if value is None else jnp.where(spot == k, picked_line, value)
        return value.astype(bf16)

    def leave(k):
        def run():
            bulk = spread[k].at[pl.ds(0, half - 1)]
            pltpu.make_async_copy(bulk, bulk, r1.at[k]).wait()
            partner = (1 - side) * half + flip(mine, 1 - side)
            if everything:
                source = spread[k]
            else:
                source = leaving[k]

                def gather(j, c):
                    sources = [asked[j * slots + i] for i in range(slots)]
                    for first, size in pieces:
                        leaving[k][j, :, first : first + size] = merge(
                            [
                                (spread[k][p // slots, :, first : first + size].astype(f32), p % slots)
                                for p in sources
                            ],
                            size,
                        )
                    return c

                lax.fori_loop(0, room // slots, gather, 0)
            pltpu.make_async_remote_copy(
                src_ref=source, dst_ref=cross[k],
                send_sem=s2.at[k], recv_sem=r2.at[k],
                device_id=at(partner), device_id_type=mesh_ids,
            ).start()

        if k < OUTER:
            run()
        else:
            pl.when(inner)(run)

    def deliver(k):
        def run():
            pltpu.make_async_copy(cross[k], cross[k], r2.at[k]).wait()
            to = pl.ds(start_of(mine, k), width)

            def pick(j):
                sources = [table[j * slots + i] for i in range(slots)]
                for first, size in pieces:
                    found = []
                    for p in sources:
                        comes = p >= split
                        a = jnp.where(comes, 0, p)
                        b = jnp.where(comes, p - split, 0)
                        x = spread[k][a // slots, :, first : first + size].astype(f32)
                        y = cross[k][b // slots, :, first : first + size].astype(f32)
                        found.append((jnp.where(comes, y, x), p % slots))
                    picked[k][j, :, first : first + size] = merge(found, size)

            def send_back(d, c):
                j = (here + d) % half
                pick(j)
                pltpu.make_async_remote_copy(
                    src_ref=picked[k].at[j], dst_ref=landed.at[:, to],
                    send_sem=s3.at[k], recv_sem=r3.at[k],
                    device_id=at(side * half + j), device_id_type=mesh_ids,
                ).start()
                return c

            lax.fori_loop(1, half, send_back, 0)
            pick(here)
            landed[:, to] = picked[k][here]

        if k < OUTER:
            run()
        else:
            pl.when(inner)(run)

    deep = slab.shape[1]
    slab_rows[:, ORB:] = jnp.zeros((slab_rows.shape[0], deep - ORB), f32)

    def chol_step(r, c):
        x = chol_ref[:, pl.ds(pl.multiple_of(r * (8 * ORB), LANES), 8 * ORB)].astype(f32)
        block = pl.ds(pl.multiple_of(r * (8 * nchol), 8), 8 * nchol)
        slab_rows[block, :ORB] = jnp.concatenate(
            [x[:, k * ORB : (k + 1) * ORB] for k in range(8)], axis=0
        )
        return c

    lax.fori_loop(0, ELEC // 8, chol_step, 0, unroll=3)
    slab[...] = slab_rows[...].astype(bf16)
    chol_copies = []
    for o in range(1, groups):
        copy = pltpu.make_async_remote_copy(
            src_ref=slab, dst_ref=other.at[o - 1],
            send_sem=sc.at[o - 1], recv_sem=rc.at[o - 1],
            device_id={"chol": (chol_index + o) % groups}, device_id_type=mesh_ids,
        )
        copy.start()
        chol_copies.append(copy)


    leave(0)
    one_rows[...] = one_ref[...].astype(f32)
    theta[ORB:] = jnp.zeros((deep - ORB, slots * LANES), bf16)

    def rows_step(r, c):
        x = padded[:, pl.ds(pl.multiple_of(r * (16 * ELEC), LANES), 16 * LANES)].astype(f32)
        for w in range(slots):
            panel_rows[w, pl.ds(r, 1), :] = x[w : w + 1]
        return c

    turns = ORB // 16
    lax.fori_loop(0, turns, rows_step, 0, unroll=5)
    part_sum = [jnp.zeros((turns, LANES), f32) for w in range(slots)]
    for t in range(15):
        o = one_rows[pl.ds(t, turns, stride=15), :]
        for w in range(slots):
            part_sum[w] = part_sum[w] + panel_rows[w, :turns, t * LANES : (t + 1) * LANES] * o
    one_part = jnp.concatenate(
        [jnp.sum(p, axis=0, keepdims=True) for p in part_sum], axis=0
    )
    one_part = jnp.sum(one_part, axis=1, keepdims=True)
    for w in range(slots):
        for q in range(16):
            theta_rows[pl.ds(w * ORB + q, turns, stride=16), :] = (
                panel_rows[w, :turns, q * ELEC : q * ELEC + LANES]
            )
    for w in range(slots):
        theta[:ORB, w * LANES : (w + 1) * LANES] = (
            theta_rows[w * ORB : (w + 1) * ORB, :].astype(bf16)
        )

    eye = (
        lax.broadcasted_iota(jnp.int32, (ELEC, ELEC), 0)
        == lax.broadcasted_iota(jnp.int32, (ELEC, ELEC), 1)
    )

    def terms(ref, carry):
        def multiply(g, c):
            block = pl.ds(pl.multiple_of(g * (2 * ELEC), 16), 2 * ELEC)
            f = jnp.dot(ref[block, :], theta[...], preferred_element_type=f32)
            for w in range(slots):
                products[w, block, :] = f[:, w * LANES : (w + 1) * LANES]
            return c

        lax.fori_loop(0, nchol // 2, multiply, 0)
        result = []
        for w in range(slots):
            square, cross = carry[w]
            for g in range(nchol):
                f = products.at[w][pl.ds(g, ELEC, stride=nchol), :][:, :ELEC]
                tr = jnp.sum(jnp.where(eye, f, 0.0), keepdims=True)
                square, cross = square + tr * tr, cross + f * f.T
            result.append((square, cross))
        return tuple(result)

    carry = tuple(
        (jnp.zeros((1, 1), f32), jnp.zeros((ELEC, ELEC), f32)) for _ in range(slots)
    )

    def announce(carry):
        for o in range(1, groups):
            chol_copies[o - 1].wait_recv()
            carry = terms(other.at[o - 1], carry)

        lane = lax.broadcasted_iota(jnp.int32, (1, LANES), 1)
        energy = jnp.zeros((1, LANES), f32)
        weights = jnp.zeros((1, LANES), f32)
        for w in range(slots):
            square, cross = carry[w]
            two_body = 0.5 * square - 0.5 * jnp.sum(cross, keepdims=True)
            energy = jnp.where(lane == w, one_part[w : w + 1] + two_body / ELEC, energy)
            weights = jnp.where(lane == w, weight_ref[w], weights)
        half_width = jnp.full((1, LANES), clip_ref[0], jnp.int32).astype(f32) / 256.0
        median = jnp.full((1, LANES), median_ref[0], f32)
        clipped = jnp.minimum(jnp.maximum(energy, median - half_width), median + half_width)
        alive = (lane < count_ref[0]) & (lane < slots)
        grown = jnp.where(alive, weights * jnp.exp(-tau_step * (clipped - median)), 0.0)
        sub = lax.broadcasted_iota(jnp.int32, (8, LANES), 0)
        messages[me] = jnp.where(
            sub == 0, grown, jnp.where(sub == 1, grown * clipped, 0.0)
        )

        def tell(d, c):
            j = (me + d) % n
            pltpu.make_async_remote_copy(
                src_ref=messages.at[me], dst_ref=messages.at[me],
                send_sem=sw, recv_sem=rw, device_id=at(j), device_id_type=mesh_ids,
            ).start()
            return c

        lax.fori_loop(1, n, tell, 0)
        for w in range(slots):
            energy_ref[w] = jnp.sum(jnp.where(lane == w, energy, 0.0))

    leave(1)
    carry = terms(slab, carry)
    leave(2)
    deliver(0)
    announce(carry)
    for k in range(3, INNER):
        leave(k)
        deliver(k - 2)
    for k in range(INNER - 2, INNER):
        deliver(k)

    heard = messages.at[pl.ds(0, n - 1)]
    pltpu.make_async_copy(heard, heard, rw).wait()
    lane = lax.broadcasted_iota(jnp.int32, (1, LANES), 1)
    every = messages[...]
    row = lax.broadcasted_iota(jnp.int32, every.shape, 1)
    holder = lax.broadcasted_iota(jnp.int32, every.shape, 0)
    lane3 = lax.broadcasted_iota(jnp.int32, every.shape, 2)
    all_grown = jnp.where(row == 0, every, 0.0)
    weight_sum = jnp.sum(jnp.sum(all_grown, axis=0), keepdims=True)
    weighted = jnp.sum(
        jnp.sum(jnp.where(row == 1, every, 0.0), axis=0), keepdims=True
    )
    estimate = weighted / weight_sum
    scale = (n * slots) / weight_sum
    fresh = jnp.zeros((1, LANES), jnp.float32)
    for w in range(slots):
        source = copy_ref[me * slots + w]
        hit = (holder * slots + lane3 == source) & (lane3 < slots)
        value = jnp.sum(
            jnp.sum(jnp.where(hit, all_grown, 0.0), axis=0), keepdims=True
        )
        fresh = jnp.where(lane == w, value * scale, fresh)
    for w in range(slots):
        fresh_ref[w] = jnp.sum(jnp.where(lane == w, fresh, 0.0))
    estimate_ref[0] = jnp.sum(jnp.where(lane == 0, estimate, 0.0))
    most = jnp.zeros((8, LANES), jnp.int32)
    if votes:
        most = counted[...]
        for o in range(1, parts):
            votes[o - 1].wait()
            most = jnp.maximum(most, told[o - 1])
    flag_ref[0] = (jnp.max(most) > room).astype(jnp.int32)
    results = [
        pltpu.make_async_copy(source, target, out.at[i])
        for i, (source, target) in enumerate((
            (energy_ref, energy_hbm), (estimate_ref, estimate_hbm),
            (fresh_ref, fresh_hbm), (flag_ref, flag_hbm),
        ))
    ]
    for copy in results:
        copy.start()

    for k in range(INNER):
        far = spread[k].at[pl.ds(0, half - 1)]
        near = spread[k].at[pl.ds(0, quarter - 1)]
        full = spread[k].at[pl.ds(0, quarter)]

        def arrived(ref):
            pltpu.make_async_copy(ref, ref, r3.at[k]).wait()

        def left(ref):
            pltpu.make_async_copy(ref, ref, s1.at[k]).wait()

        def done():
            pltpu.make_async_copy(cross[k], cross[k], s2.at[k]).wait()
            pltpu.make_async_copy(far, far, s3.at[k]).wait()

        if k < OUTER:
            arrived(far)
            left(far)
            done()
        else:

            @pl.when(inner)
            def _():
                arrived(near)
                left(near)
                done()

            @pl.when(mine >= quarter)
            def _():
                arrived(full)
                left(full)

    for copy in chol_copies:
        copy.wait_send()
    pltpu.make_async_copy(heard, heard, sw).wait()
    for copy in results:
        copy.wait()


CHUNKS = 8


def finish(*refs):
    sources, targets, sems = refs[:4], refs[4:8], refs[8]
    panel_ref, out_ref = sources[0], targets[0]
    tiles = out_ref.shape[1] // LANES
    copies = []
    for i in range(CHUNKS):
        first, end = tiles * i // CHUNKS, tiles * (i + 1) // CHUNKS
        chunk = pl.ds(first * LANES, (end - first) * LANES)
        copies.append(
            pltpu.make_async_copy(panel_ref.at[:, chunk], out_ref.at[:, chunk], sems.at[i])
        )
    for i in range(1, 4):
        copies.append(
            pltpu.make_async_copy(sources[i], targets[i], sems.at[CHUNKS - 1 + i])
        )
    for copy in copies:
        copy.start()
    for copy in copies:
        copy.wait()


def per_device(green, chol_vecs, one_body, weights, counts, copy_list, e_median, clip_bin):
    slots, length = green.shape
    nchol = chol_vecs.shape[0]
    groups = lax.axis_size("chol")
    n = lax.axis_size("walk") * groups
    parts = lax.axis_size("ens")
    tiles = length // LANES
    units, unit = layout(n, groups, tiles)
    width = unit * LANES
    half = n // 2
    deep = -(-ORB // 256) * 256
    wide = max(units * unit, tiles + 1) * LANES
    bf16, f32 = jnp.bfloat16, jnp.float32
    vmem = pl.BlockSpec(memory_space=pltpu.VMEM)
    smem = pl.BlockSpec(memory_space=pltpu.SMEM)
    hbm = pl.BlockSpec(memory_space=pltpu.HBM)
    dma = pltpu.SemaphoreType.DMA

    operands = (
        copy_list, weights, e_median, counts, clip_bin,
        green, chol_vecs, one_body.reshape(tiles, LANES),
    )
    numbers = [
        jax.ShapeDtypeStruct((slots,), f32),
        jax.ShapeDtypeStruct((1,), f32),
        jax.ShapeDtypeStruct((slots,), f32),
    ]

    def run(room, number, *operands):
        def buffer(rows):
            return [pltpu.VMEM((rows, slots, width), bf16)] * INNER

        spare = [pltpu.VMEM((1, slots, LANES), bf16)] * INNER
        return pl.pallas_call(
            functools.partial(body, n, groups, unit, room),
            out_shape=(
                jax.ShapeDtypeStruct((slots, wide), bf16),
                *numbers,
                jax.ShapeDtypeStruct((1,), jnp.int32),
            ),
            in_specs=[hbm] * 8,
            out_specs=(vmem, hbm, hbm, hbm, hbm),
            scratch_shapes=[
                    pltpu.VMEM((slots, wide), bf16),
                    pltpu.VMEM((nchol * ELEC, deep), bf16),
                    pltpu.VMEM((groups - 1, nchol * ELEC, deep), bf16),
                    pltpu.VMEM((n, 8, LANES), f32),
                    pltpu.VMEM((slots, -(-(ORB // 16) // 8) * 8, 16 * LANES), f32),
                    pltpu.VMEM((slots * ORB, LANES), f32),
                    pltpu.VMEM((deep, slots * LANES), bf16),
                    pltpu.VMEM((nchol * ELEC, deep), f32),
                    pltpu.VMEM((slots, nchol * ELEC, LANES), f32),
                    pltpu.VMEM((tiles, LANES), f32),
                    pltpu.VMEM(chol_vecs.shape, bf16),
                    pltpu.VMEM((tiles, LANES), bf16),
                    pltpu.SMEM(copy_list.shape, jnp.int32),
                    pltpu.SMEM(weights.shape, f32),
                    pltpu.SMEM((1,), f32),
                    pltpu.SMEM((1,), jnp.int32),
                    pltpu.SMEM((1,), jnp.int32),
                    pltpu.SMEM((half * slots,), jnp.int32),
                    pltpu.SMEM((room,), jnp.int32),
                    pltpu.VMEM((8, LANES), jnp.int32),
                    pltpu.VMEM((parts - 1, 8, LANES), jnp.int32),
                    pltpu.SMEM((slots,), f32),
                    pltpu.SMEM((1,), f32),
                    pltpu.SMEM((slots,), f32),
                    pltpu.SMEM((1,), jnp.int32),
                    dma((8,)), dma((parts - 1,)), dma((parts - 1,)), dma((4,)),
                    dma((INNER,)), dma((INNER,)), dma((INNER,)), dma((INNER,)),
                    dma((INNER,)), dma((INNER,)),
                    dma((groups - 1,)), dma((groups - 1,)), dma, dma,
                    *buffer(half), *buffer(room // slots),
                    *(buffer(room // slots) if room < half * slots else spare),
                    *buffer(half),
            ],
            compiler_params=pltpu.CompilerParams(
                collective_id=number, has_side_effects=True,
                vmem_limit_bytes=60 * 1024 * 1024,
            ),
        )(*operands)

    def hand_over(panels, energy, estimate, fresh):
        out, *rest = pl.pallas_call(
            finish,
            out_shape=(jax.ShapeDtypeStruct((slots, length), bf16), *numbers),
            in_specs=[vmem, hbm, hbm, hbm],
            out_specs=(hbm,) * 4,
            scratch_shapes=[dma((CHUNKS + 3,))],
        )(panels, energy, estimate, fresh)
        return *rest, out

    *first, flag = run(min(ROOM, half * slots), 0, *operands)
    return lax.cond(
        flag[0] == 0,
        lambda first, operands: hand_over(*first),
        lambda first, operands: hand_over(*run(half * slots, 1, *operands)[:4]),
        first, operands,
    )


def solution(mesh):
    placed = (
        P(("ens", "walk", "chol"), None),
        P("chol", None),
        P(),
        P(("ens", "walk", "chol")),
        P(("ens", "walk", "chol")),
        P("ens"),
        P("ens"),
        P("ens"),
    )
    return jax.shard_map(
        per_device,
        mesh=mesh,
        in_specs=placed,
        out_specs=(
            P(("ens", "walk", "chol")),
            P("ens"),
            P(("ens", "walk", "chol")),
            P(("ens", "walk", "chol"), None),
        ),
        check_vma=False,
    )
```

```python
import functools

import jax
import jax.numpy as jnp
from jax import lax
from jax.experimental import pallas as pl
from jax.experimental.pallas import tpu as pltpu
from jax.sharding import PartitionSpec as P

ORB = 1200
ELEC = 120
LANES = 128
STEPS = 4
LINE = 2
ROOM = 8


tau_step = 0.2


def body(
    n, groups, unit, room,
    copy_hbm, weight_hbm, count_hbm,
    panel_ref, chol_hbm, one_hbm,
    landed, messages, flag_hbm,
    padded, slab, other,
    panel_rows, theta_rows, theta, slab_rows, products, one_rows,
    chol_ref, one_ref, copy_ref, weight_ref, count_ref,
    table, asked, counted, told, flag_ref,
    lp, local, sv, rv, out, s1, r1, s2, r2, s3, r3, sc, rc, sw, rw,
    *buffers,
):
    slots, length = panel_ref.shape
    nchol = chol_ref.shape[0]
    half = n // 2
    width = unit * LANES
    spread, cross, leaving, picked = [
        buffers[i * STEPS : (i + 1) * STEPS] for i in range(4)
    ]
    everything = room >= half * slots
    chol_index = lax.axis_index("chol")
    me = lax.axis_index("walk") * groups + chol_index
    side, here = lax.div(me, half), lax.rem(me, half)
    parts, part = lax.axis_size("ens"), lax.axis_index("ens")
    mesh_ids = pl.DeviceIdType.MESH
    f32, bf16 = jnp.float32, jnp.bfloat16

    def at(j):
        return {"walk": lax.div(j, groups), "chol": lax.rem(j, groups)}

    def mirror(h):
        return half - LINE * groups * (1 + lax.div(h, LINE * groups)) + lax.rem(h, LINE * groups)

    across = mirror(here)

    def place(h, k):
        h = jnp.where(side == 0, h, mirror(h))
        return pl.ds(pl.multiple_of((k * half + h) * width, LANES), width)

    barrier = pltpu.get_barrier_semaphore()
    panel_fetches = []
    for k in range(STEPS):
        first = min(k * half * width, length)
        part_of = pl.ds(first, min((k + 1) * half * width, length) - first)
        if first < length:
            fetch = pltpu.make_async_copy(
                panel_ref.at[:, part_of], padded.at[:, part_of], lp.at[k]
            )
            fetch.start()
            panel_fetches.append(fetch)

    def greet(d, c):
        pl.semaphore_signal(
            barrier, inc=1, device_id=at(lax.rem(me + d, n)), device_id_type=mesh_ids
        )
        return c

    lax.fori_loop(1, n, greet, 0)
    for o in range(1, parts):
        pl.semaphore_signal(
            barrier, inc=1, device_id={"ens": (part + o) % parts}, device_id_type=mesh_ids
        )
    fetches = [
        pltpu.make_async_copy(source, target, local.at[1 + i])
        for i, (source, target) in enumerate((
            (chol_hbm, chol_ref), (one_hbm, one_ref), (copy_hbm, copy_ref),
            (weight_hbm, weight_ref), (count_hbm, count_ref),
        ))
    ]
    for copy in fetches:
        copy.start()
    padded[:, length:] = jnp.zeros((slots, padded.shape[1] - length), bf16)
    pl.semaphore_wait(barrier, n - 1 + parts - 1)

    for k in range(STEPS):
        for fetch in panel_fetches[k : k + 1]:
            fetch.wait()

        def send_slice(d, c):
            h = lax.rem(here + d, half)
            pltpu.make_async_remote_copy(
                src_ref=padded.at[:, place(h, k)], dst_ref=spread[k].at[here],
                send_sem=s1.at[k], recv_sem=r1.at[k],
                device_id=at(side * half + h), device_id_type=mesh_ids,
            ).start()
            return c

        lax.fori_loop(1, half, send_slice, 0)
    for k in range(STEPS):
        spread[k][here] = padded[:, place(here, k)]
    for copy in fetches:
        copy.wait()

    split = half * slots
    base, away = side * split, (1 - side) * split

    def read_own(d, carry):
        before, rank = carry
        source = copy_ref[base + d]
        comes = source // split != side
        fresh = comes & (source != before)
        rank = rank + fresh.astype(jnp.int32)
        place = source - away if everything else jnp.minimum(rank - 1, room - 1)
        table[d] = jnp.where(comes, split + place, source - base)
        return source, rank

    arriving = lax.fori_loop(0, split, read_own, (jnp.int32(-1), jnp.int32(0)))[1]
    votes = []
    if not everything:

        def read_away(d, carry):
            before, rank, chosen = carry
            source = copy_ref[away + d]
            fresh = (source // split == side) & (source != before)
            chosen = tuple(
                jnp.where(fresh & (rank == m), source - base, chosen[m])
                for m in range(room)
            )
            return source, rank + fresh.astype(jnp.int32), chosen

        _, departing, chosen = lax.fori_loop(
            0, split, read_away,
            (jnp.int32(-1), jnp.int32(0), (jnp.int32(0),) * room),
        )
        for m in range(room):
            asked[m] = chosen[m]
        counted[...] = jnp.full(counted.shape, jnp.maximum(arriving, departing), jnp.int32)
        for o in range(1, parts):
            vote = pltpu.make_async_remote_copy(
                src_ref=counted, dst_ref=told.at[o - 1],
                send_sem=sv.at[o - 1], recv_sem=rv.at[o - 1],
                device_id={"ens": (part + o) % parts}, device_id_type=mesh_ids,
            )
            vote.start()
            votes.append(vote)

    step = 8 * LANES
    pieces = [(f, min(step, width - f)) for f in range(0, width, step)]

    def merge(lines_of, size):
        spot = lax.broadcasted_iota(jnp.int32, (slots, size), 0)
        value = None
        for k, (x, row) in enumerate(lines_of):
            picked_line = x[0:1]
            for w in range(1, slots):
                picked_line = jnp.where(row == w, x[w : w + 1], picked_line)
            picked_line = jnp.broadcast_to(picked_line, (slots, size))
            value = picked_line if value is None else jnp.where(spot == k, picked_line, value)
        return value.astype(bf16)

    def leave(k):
        bulk = spread[k].at[pl.ds(0, half - 1)]
        pltpu.make_async_copy(bulk, bulk, r1.at[k]).wait()
        source = spread[k]
        if not everything:
            source = leaving[k]

            def gather(j, c):
                sources = [asked[j * slots + i] for i in range(slots)]
                for first, size in pieces:
                    leaving[k][j, :, first : first + size] = merge(
                        [
                            (spread[k][p // slots, :, first : first + size].astype(f32), p % slots)
                            for p in sources
                        ],
                        size,
                    )
                return c

            lax.fori_loop(0, room // slots, gather, 0)
        pltpu.make_async_remote_copy(
            src_ref=source, dst_ref=cross[k],
            send_sem=s2.at[k], recv_sem=r2.at[k],
            device_id=at((1 - side) * half + across), device_id_type=mesh_ids,
        ).start()

    def deliver(k):
        pltpu.make_async_copy(cross[k], cross[k], r2.at[k]).wait()
        to = place(here, k)

        def pick(j):
            sources = [table[j * slots + i] for i in range(slots)]
            for first, size in pieces:
                found = []
                for p in sources:
                    comes = p >= split
                    a = jnp.where(comes, 0, p)
                    b = jnp.where(comes, p - split, 0)
                    x = spread[k][a // slots, :, first : first + size].astype(f32)
                    y = cross[k][b // slots, :, first : first + size].astype(f32)
                    found.append((jnp.where(comes, y, x), p % slots))
                picked[k][j, :, first : first + size] = merge(found, size)

        def send_back(d, c):
            j = lax.rem(here + d, half)
            pick(j)
            pltpu.make_async_remote_copy(
                src_ref=picked[k].at[j], dst_ref=landed.at[:, to],
                send_sem=s3.at[k], recv_sem=r3.at[k],
                device_id=at(side * half + j), device_id_type=mesh_ids,
            ).start()
            return c

        lax.fori_loop(1, half, send_back, 0)
        pick(here)
        landed[:, to] = picked[k][here]

    deep = slab.shape[1]
    slab_rows[:, ORB:] = jnp.zeros((slab_rows.shape[0], deep - ORB), f32)

    def chol_step(r, c):
        x = chol_ref[:, pl.ds(pl.multiple_of(r * (8 * ORB), LANES), 8 * ORB)].astype(f32)
        block = pl.ds(pl.multiple_of(r * (8 * nchol), 8), 8 * nchol)
        slab_rows[block, :ORB] = jnp.concatenate(
            [x[:, k * ORB : (k + 1) * ORB] for k in range(8)], axis=0
        )
        return c

    lax.fori_loop(0, ELEC // 8, chol_step, 0, unroll=3)
    slab[...] = slab_rows[...].astype(bf16)
    chol_copies = []
    for o in range(1, groups):
        copy = pltpu.make_async_remote_copy(
            src_ref=slab, dst_ref=other.at[o - 1],
            send_sem=sc.at[o - 1], recv_sem=rc.at[o - 1],
            device_id={"chol": (chol_index + o) % groups}, device_id_type=mesh_ids,
        )
        copy.start()
        chol_copies.append(copy)


    leave(0)
    one_rows[...] = one_ref[...].astype(f32)
    theta[ORB:] = jnp.zeros((deep - ORB, slots * LANES), bf16)

    def rows_step(r, c):
        x = padded[:, pl.ds(pl.multiple_of(r * (16 * ELEC), LANES), 16 * LANES)].astype(f32)
        for w in range(slots):
            panel_rows[w, pl.ds(r, 1), :] = x[w : w + 1]
        return c

    turns = ORB // 16
    lax.fori_loop(0, turns, rows_step, 0, unroll=5)
    part_sum = [jnp.zeros((turns, LANES), f32) for w in range(slots)]
    for t in range(15):
        o = one_rows[pl.ds(t, turns, stride=15), :]
        for w in range(slots):
            part_sum[w] = part_sum[w] + panel_rows[w, :turns, t * LANES : (t + 1) * LANES] * o
    one_part = jnp.concatenate(
        [jnp.sum(p, axis=0, keepdims=True) for p in part_sum], axis=0
    )
    one_part = jnp.sum(one_part, axis=1, keepdims=True)
    for w in range(slots):
        for q in range(16):
            theta_rows[pl.ds(w * ORB + q, turns, stride=16), :] = (
                panel_rows[w, :turns, q * ELEC : q * ELEC + LANES]
            )
    for w in range(slots):
        theta[:ORB, w * LANES : (w + 1) * LANES] = (
            theta_rows[w * ORB : (w + 1) * ORB, :].astype(bf16)
        )

    eye = (
        lax.broadcasted_iota(jnp.int32, (ELEC, ELEC), 0)
        == lax.broadcasted_iota(jnp.int32, (ELEC, ELEC), 1)
    )

    def terms(ref, carry):
        def multiply(g, c):
            block = pl.ds(pl.multiple_of(g * (2 * ELEC), 16), 2 * ELEC)
            f = jnp.dot(ref[block, :], theta[...], preferred_element_type=f32)
            for w in range(slots):
                products[w, block, :] = f[:, w * LANES : (w + 1) * LANES]
            return c

        lax.fori_loop(0, nchol // 2, multiply, 0)
        result = []
        for w in range(slots):
            square, cross = carry[w]
            for g in range(nchol):
                f = products.at[w][pl.ds(g, ELEC, stride=nchol), :][:, :ELEC]
                tr = jnp.sum(jnp.where(eye, f, 0.0), keepdims=True)
                square, cross = square + tr * tr, cross + f * f.T
            result.append((square, cross))
        return tuple(result)

    carry = tuple(
        (jnp.zeros((1, 1), f32), jnp.zeros((ELEC, ELEC), f32)) for _ in range(slots)
    )

    def announce(carry):
        for o in range(1, groups):
            chol_copies[o - 1].wait_recv()
            carry = terms(other.at[o - 1], carry)

        lane = lax.broadcasted_iota(jnp.int32, (1, LANES), 1)
        energy = jnp.zeros((1, LANES), f32)
        weights = jnp.zeros((1, LANES), f32)
        for w in range(slots):
            square, cross = carry[w]
            two_body = 0.5 * square - 0.5 * jnp.sum(cross, keepdims=True)
            energy = jnp.where(lane == w, one_part[w : w + 1] + two_body / ELEC, energy)
            weights = jnp.where(lane == w, weight_ref[w], weights)
        alive = (lane < count_ref[0]) & (lane < slots)
        sub = lax.broadcasted_iota(jnp.int32, (8, LANES), 0)
        messages[me] = jnp.where(
            sub == 0, energy, jnp.where((sub == 1) & alive, weights, 0.0)
        )

        def tell(d, c):
            j = (me + d) % n
            pltpu.make_async_remote_copy(
                src_ref=messages.at[me], dst_ref=messages.at[me],
                send_sem=sw, recv_sem=rw, device_id=at(j), device_id_type=mesh_ids,
            ).start()
            return c

        lax.fori_loop(1, n, tell, 0)

    leave(1)
    carry = terms(slab, carry)
    leave(2)
    deliver(0)
    announce(carry)
    most = jnp.zeros((8, LANES), jnp.int32)
    if votes:
        most = counted[...]
        for o in range(1, parts):
            votes[o - 1].wait()
            most = jnp.maximum(most, told[o - 1])
    flag_ref[0] = (jnp.max(most) > room).astype(jnp.int32)
    flag_copy = pltpu.make_async_copy(flag_ref, flag_hbm, out)
    flag_copy.start()
    for k in range(3, STEPS):
        leave(k)
        deliver(k - 2)
    for k in range(STEPS - 2, STEPS):
        deliver(k)

    heard = messages.at[pl.ds(0, n - 1)]
    pltpu.make_async_copy(heard, heard, rw).wait()
    for k in range(STEPS):
        bulk = spread[k].at[pl.ds(0, half - 1)]
        pltpu.make_async_copy(bulk, bulk, r3.at[k]).wait()
        pltpu.make_async_copy(bulk, bulk, s1.at[k]).wait()
        pltpu.make_async_copy(cross[k], cross[k], s2.at[k]).wait()
        pltpu.make_async_copy(bulk, bulk, s3.at[k]).wait()

    for copy in chol_copies:
        copy.wait_send()
    pltpu.make_async_copy(heard, heard, sw).wait()
    flag_copy.wait()


CHUNKS = 1


def finish(
    panel_ref, messages, copy_ref, median_ref, clip_ref,
    energy_hbm, estimate_hbm, fresh_hbm, out_ref,
    energy_ref, estimate_ref, fresh_ref, sems,
):
    n, slots = messages.shape[0], out_ref.shape[0]
    me = lax.axis_index("walk") * lax.axis_size("chol") + lax.axis_index("chol")
    f32 = jnp.float32
    tiles = out_ref.shape[1] // LANES
    copies = []
    for i in range(CHUNKS):
        first, end = tiles * i // CHUNKS, tiles * (i + 1) // CHUNKS
        chunk = pl.ds(first * LANES, (end - first) * LANES)
        copy = pltpu.make_async_copy(
            panel_ref.at[:, chunk], out_ref.at[:, chunk], sems.at[i]
        )
        copy.start()
        copies.append(copy)
    lane = lax.broadcasted_iota(jnp.int32, (1, LANES), 1)
    energy, live = messages[:, 0, :], messages[:, 1, :]
    for w in range(slots):
        energy_ref[w] = jnp.sum(jnp.where(lane == w, messages[me][0:1], 0.0))
    wanted = copy_ref[...].reshape(1, -1)
    slot = lax.broadcasted_iota(jnp.int32, wanted.shape, 1)
    sources = [
        jnp.sum(jnp.where(slot == me * slots + w, wanted, 0), axis=1, keepdims=True)
        for w in range(slots)
    ]
    half_width = jnp.broadcast_to(clip_ref[...].reshape(1, 1), (n, LANES)).astype(f32) / 256.0
    median = jnp.broadcast_to(median_ref[...].reshape(1, 1), (n, LANES))
    clipped = jnp.minimum(jnp.maximum(energy, median - half_width), median + half_width)
    grown = jnp.where(live > 0.0, live * jnp.exp(-tau_step * (clipped - median)), 0.0)
    place = lax.broadcasted_iota(jnp.int32, (n, LANES), 0) * slots
    column = lax.broadcasted_iota(jnp.int32, (n, LANES), 1)
    place = jnp.where(column < slots, place + column, -1)
    weight_sum = jnp.sum(grown, keepdims=True)
    weighted = jnp.sum(grown * clipped, keepdims=True)
    copied = [
        jnp.sum(jnp.where(place == source, grown, 0.0), keepdims=True) for source in sources
    ]
    scale = (n * slots) / weight_sum
    estimate_ref[0] = (weighted / weight_sum)[0, 0]
    for w in range(slots):
        fresh_ref[w] = (copied[w] * scale)[0, 0]
    results = [
        pltpu.make_async_copy(source, target, sems.at[CHUNKS + i])
        for i, (source, target) in enumerate((
            (energy_ref, energy_hbm), (estimate_ref, estimate_hbm), (fresh_ref, fresh_hbm),
        ))
    ]
    for copy in results:
        copy.start()
    for copy in copies + results:
        copy.wait()


def per_device(green, chol_vecs, one_body, weights, counts, copy_list, e_median, clip_bin):
    slots, length = green.shape
    nchol = chol_vecs.shape[0]
    groups = lax.axis_size("chol")
    n = lax.axis_size("walk") * groups
    parts = lax.axis_size("ens")
    tiles = length // LANES
    units = n // 2 * STEPS
    unit = -(-tiles // units)
    width = unit * LANES
    half = n // 2
    deep = -(-ORB // 256) * 256
    wide = max(units * unit, tiles + 1) * LANES
    bf16, f32 = jnp.bfloat16, jnp.float32
    vmem = pl.BlockSpec(memory_space=pltpu.VMEM)
    smem = pl.BlockSpec(memory_space=pltpu.SMEM)
    hbm = pl.BlockSpec(memory_space=pltpu.HBM)
    dma = pltpu.SemaphoreType.DMA

    operands = (
        copy_list, weights, counts,
        green, chol_vecs, one_body.reshape(tiles, LANES),
    )
    def run(room, number, *operands):
        def buffer(rows):
            return [pltpu.VMEM((rows, slots, width), bf16)] * STEPS

        spare = [pltpu.VMEM((1, slots, LANES), bf16)] * STEPS
        return pl.pallas_call(
            functools.partial(body, n, groups, unit, room),
            out_shape=(
                jax.ShapeDtypeStruct((slots, wide), bf16),
                jax.ShapeDtypeStruct((n, 8, LANES), f32),
                jax.ShapeDtypeStruct((1,), jnp.int32),
            ),
            in_specs=[hbm] * 6,
            out_specs=(vmem, vmem, hbm),
            scratch_shapes=[
                    pltpu.VMEM((slots, wide), bf16),
                    pltpu.VMEM((nchol * ELEC, deep), bf16),
                    pltpu.VMEM((groups - 1, nchol * ELEC, deep), bf16),
                    pltpu.VMEM((slots, -(-(ORB // 16) // 8) * 8, 16 * LANES), f32),
                    pltpu.VMEM((slots * ORB, LANES), f32),
                    pltpu.VMEM((deep, slots * LANES), bf16),
                    pltpu.VMEM((nchol * ELEC, deep), f32),
                    pltpu.VMEM((slots, nchol * ELEC, LANES), f32),
                    pltpu.VMEM((tiles, LANES), f32),
                    pltpu.VMEM(chol_vecs.shape, bf16),
                    pltpu.VMEM((tiles, LANES), bf16),
                    pltpu.SMEM(copy_list.shape, jnp.int32),
                    pltpu.SMEM(weights.shape, f32),
                    pltpu.SMEM((1,), jnp.int32),
                    pltpu.SMEM((half * slots,), jnp.int32),
                    pltpu.SMEM((room,), jnp.int32),
                    pltpu.VMEM((8, LANES), jnp.int32),
                    pltpu.VMEM((parts - 1, 8, LANES), jnp.int32),
                    pltpu.SMEM((1,), jnp.int32),
                    dma((STEPS,)), dma((8,)), dma((parts - 1,)), dma((parts - 1,)), dma,
                    *[dma((STEPS,))] * 6,
                    dma((groups - 1,)), dma((groups - 1,)), dma, dma,
                    *buffer(half), *buffer(room // slots),
                    *(buffer(room // slots) if room < half * slots else spare),
                    *buffer(half),
            ],
            compiler_params=pltpu.CompilerParams(
                collective_id=number, has_side_effects=True,
                vmem_limit_bytes=60 * 1024 * 1024,
            ),
        )(*operands)

    def hand_over(panels, messages):
        return pl.pallas_call(
            finish,
            out_shape=(
                jax.ShapeDtypeStruct((slots,), f32),
                jax.ShapeDtypeStruct((1,), f32),
                jax.ShapeDtypeStruct((slots,), f32),
                jax.ShapeDtypeStruct((slots, length), bf16),
            ),
            in_specs=[vmem] * 5,
            out_specs=(hbm,) * 4,
            scratch_shapes=[
                pltpu.SMEM((slots,), f32),
                pltpu.SMEM((1,), f32),
                pltpu.SMEM((slots,), f32),
                dma((CHUNKS + 3,)),
            ],
        )(panels, messages, copy_list, e_median, clip_bin)

    panels, messages, flag = run(min(ROOM, half * slots), 0, *operands)
    return lax.switch(
        flag[0],
        (
            lambda panels, messages, *operands: hand_over(panels, messages),
            lambda panels, messages, *operands: hand_over(
                *run(half * slots, 1, *operands)[:2]
            ),
        ),
        panels, messages, *operands,
    )


def solution(mesh):
    placed = (
        P(("ens", "walk", "chol"), None),
        P("chol", None),
        P(),
        P(("ens", "walk", "chol")),
        P(("ens", "walk", "chol")),
        P("ens"),
        P("ens"),
        P("ens"),
    )
    return jax.shard_map(
        per_device,
        mesh=mesh,
        in_specs=placed,
        out_specs=(
            P(("ens", "walk", "chol")),
            P("ens"),
            P(("ens", "walk", "chol")),
            P(("ens", "walk", "chol"), None),
        ),
        check_vma=False,
    )
```

```python
import functools

import jax
import jax.numpy as jnp
from jax import lax
from jax.experimental import pallas as pl
from jax.experimental.pallas import tpu as pltpu
from jax.sharding import PartitionSpec as P

ORB = 1200
ELEC = 120
LANES = 128
STEPS = 4
LINE = 2
ROOM = 8


tau_step = 0.2


def body(
    n, groups, unit, room,
    copy_hbm, weight_hbm, count_hbm,
    panel_ref, chol_hbm, one_hbm,
    landed, messages, flag_hbm,
    padded, slab, other,
    panel_rows, theta_rows, theta, slab_rows, products, one_rows,
    chol_ref, one_ref, copy_ref, weight_ref, count_ref,
    table, asked, counted, told, flag_ref,
    lp, local, sv, rv, out, s1, r1, s2, r2, s3, r3, sc, rc, sw, rw,
    *buffers,
):
    slots, length = panel_ref.shape
    nchol = chol_ref.shape[0]
    half = n // 2
    width = unit * LANES
    spread, cross, leaving, picked = [
        buffers[i * STEPS : (i + 1) * STEPS] for i in range(4)
    ]
    everything = room >= half * slots
    chol_index = lax.axis_index("chol")
    me = lax.axis_index("walk") * groups + chol_index
    side, here = lax.div(me, half), lax.rem(me, half)
    parts, part = lax.axis_size("ens"), lax.axis_index("ens")
    mesh_ids = pl.DeviceIdType.MESH
    f32, bf16 = jnp.float32, jnp.bfloat16

    def at(j):
        return {"walk": lax.div(j, groups), "chol": lax.rem(j, groups)}

    def mirror(h):
        return half - LINE * groups * (1 + lax.div(h, LINE * groups)) + lax.rem(h, LINE * groups)

    across = mirror(here)

    def place(h, k):
        h = jnp.where(side == 0, h, mirror(h))
        return pl.ds(pl.multiple_of((k * half + h) * width, LANES), width)

    barrier = pltpu.get_barrier_semaphore()
    panel_fetches = []
    for k in range(STEPS):
        first = min(k * half * width, length)
        part_of = pl.ds(first, min((k + 1) * half * width, length) - first)
        if first < length:
            fetch = pltpu.make_async_copy(
                panel_ref.at[:, part_of], padded.at[:, part_of], lp.at[k]
            )
            fetch.start()
            panel_fetches.append(fetch)

    def greet(d, c):
        pl.semaphore_signal(
            barrier, inc=1, device_id=at(lax.rem(me + d, n)), device_id_type=mesh_ids
        )
        return c

    lax.fori_loop(1, n, greet, 0)
    for o in range(1, parts):
        pl.semaphore_signal(
            barrier, inc=1, device_id={"ens": (part + o) % parts}, device_id_type=mesh_ids
        )
    fetches = [
        pltpu.make_async_copy(source, target, local.at[1 + i])
        for i, (source, target) in enumerate((
            (chol_hbm, chol_ref), (one_hbm, one_ref), (copy_hbm, copy_ref),
            (weight_hbm, weight_ref), (count_hbm, count_ref),
        ))
    ]
    for copy in fetches:
        copy.start()
    padded[:, length:] = jnp.zeros((slots, padded.shape[1] - length), bf16)
    pl.semaphore_wait(barrier, n - 1 + parts - 1)

    for k in range(STEPS):
        for fetch in panel_fetches[k : k + 1]:
            fetch.wait()

        def send_slice(d, c):
            h = lax.rem(here + d, half)
            pltpu.make_async_remote_copy(
                src_ref=padded.at[:, place(h, k)], dst_ref=spread[k].at[here],
                send_sem=s1.at[k], recv_sem=r1.at[k],
                device_id=at(side * half + h), device_id_type=mesh_ids,
            ).start()
            return c

        lax.fori_loop(1, half, send_slice, 0)
    for k in range(STEPS):
        spread[k][here] = padded[:, place(here, k)]
    for copy in fetches:
        copy.wait()

    split = half * slots
    base, away = side * split, (1 - side) * split

    def read_own(d, carry):
        before, rank = carry
        source = copy_ref[base + d]
        comes = source // split != side
        fresh = comes & (source != before)
        rank = rank + fresh.astype(jnp.int32)
        place = source - away if everything else jnp.minimum(rank - 1, room - 1)
        table[d] = jnp.where(comes, split + place, source - base)
        return source, rank

    arriving = lax.fori_loop(0, split, read_own, (jnp.int32(-1), jnp.int32(0)))[1]
    votes = []
    if not everything:

        def read_away(d, carry):
            before, rank, chosen = carry
            source = copy_ref[away + d]
            fresh = (source // split == side) & (source != before)
            chosen = tuple(
                jnp.where(fresh & (rank == m), source - base, chosen[m])
                for m in range(room)
            )
            return source, rank + fresh.astype(jnp.int32), chosen

        _, departing, chosen = lax.fori_loop(
            0, split, read_away,
            (jnp.int32(-1), jnp.int32(0), (jnp.int32(0),) * room),
        )
        for m in range(room):
            asked[m] = chosen[m]
        counted[...] = jnp.full(counted.shape, jnp.maximum(arriving, departing), jnp.int32)
        for o in range(1, parts):
            vote = pltpu.make_async_remote_copy(
                src_ref=counted, dst_ref=told.at[o - 1],
                send_sem=sv.at[o - 1], recv_sem=rv.at[o - 1],
                device_id={"ens": (part + o) % parts}, device_id_type=mesh_ids,
            )
            vote.start()
            votes.append(vote)

    step = 8 * LANES
    pieces = [(f, min(step, width - f)) for f in range(0, width, step)]

    def merge(lines_of, size):
        spot = lax.broadcasted_iota(jnp.int32, (slots, size), 0)
        value = None
        for k, (x, row) in enumerate(lines_of):
            picked_line = x[0:1]
            for w in range(1, slots):
                picked_line = jnp.where(row == w, x[w : w + 1], picked_line)
            picked_line = jnp.broadcast_to(picked_line, (slots, size))
            value = picked_line if value is None else jnp.where(spot == k, picked_line, value)
        return value.astype(bf16)

    def leave(k):
        bulk = spread[k].at[pl.ds(0, half - 1)]
        pltpu.make_async_copy(bulk, bulk, r1.at[k]).wait()
        source = spread[k]
        if not everything:
            source = leaving[k]

            def gather(j, c):
                sources = [asked[j * slots + i] for i in range(slots)]
                for first, size in pieces:
                    leaving[k][j, :, first : first + size] = merge(
                        [
                            (spread[k][p // slots, :, first : first + size].astype(f32), p % slots)
                            for p in sources
                        ],
                        size,
                    )
                return c

            lax.fori_loop(0, room // slots, gather, 0)
        pltpu.make_async_remote_copy(
            src_ref=source, dst_ref=cross[k],
            send_sem=s2.at[k], recv_sem=r2.at[k],
            device_id=at((1 - side) * half + across), device_id_type=mesh_ids,
        ).start()

    def deliver(k):
        pltpu.make_async_copy(cross[k], cross[k], r2.at[k]).wait()
        to = place(here, k)

        def pick(j):
            sources = [table[j * slots + i] for i in range(slots)]
            for first, size in pieces:
                found = []
                for p in sources:
                    comes = p >= split
                    a = jnp.where(comes, 0, p)
                    b = jnp.where(comes, p - split, 0)
                    x = spread[k][a // slots, :, first : first + size].astype(f32)
                    y = cross[k][b // slots, :, first : first + size].astype(f32)
                    found.append((jnp.where(comes, y, x), p % slots))
                picked[k][j, :, first : first + size] = merge(found, size)

        def send_back(d, c):
            j = lax.rem(here + d, half)
            pick(j)
            pltpu.make_async_remote_copy(
                src_ref=picked[k].at[j], dst_ref=landed.at[:, to],
                send_sem=s3.at[k], recv_sem=r3.at[k],
                device_id=at(side * half + j), device_id_type=mesh_ids,
            ).start()
            return c

        lax.fori_loop(1, half, send_back, 0)
        pick(here)
        landed[:, to] = picked[k][here]

    deep = slab.shape[1]
    slab_rows[:, ORB:] = jnp.zeros((slab_rows.shape[0], deep - ORB), f32)

    def chol_step(r, c):
        x = chol_ref[:, pl.ds(pl.multiple_of(r * (8 * ORB), LANES), 8 * ORB)].astype(f32)
        block = pl.ds(pl.multiple_of(r * (8 * nchol), 8), 8 * nchol)
        slab_rows[block, :ORB] = jnp.concatenate(
            [x[:, k * ORB : (k + 1) * ORB] for k in range(8)], axis=0
        )
        return c

    lax.fori_loop(0, ELEC // 8, chol_step, 0, unroll=3)
    slab[...] = slab_rows[...].astype(bf16)
    chol_copies = []
    for o in range(1, groups):
        copy = pltpu.make_async_remote_copy(
            src_ref=slab, dst_ref=other.at[o - 1],
            send_sem=sc.at[o - 1], recv_sem=rc.at[o - 1],
            device_id={"chol": (chol_index + o) % groups}, device_id_type=mesh_ids,
        )
        copy.start()
        chol_copies.append(copy)


    leave(0)
    one_rows[...] = one_ref[...].astype(f32)
    theta[ORB:] = jnp.zeros((deep - ORB, slots * LANES), bf16)

    def rows_step(r, c):
        x = padded[:, pl.ds(pl.multiple_of(r * (16 * ELEC), LANES), 16 * LANES)].astype(f32)
        for w in range(slots):
            panel_rows[w, pl.ds(r, 1), :] = x[w : w + 1]
        return c

    turns = ORB // 16
    lax.fori_loop(0, turns, rows_step, 0, unroll=5)
    part_sum = [jnp.zeros((turns, LANES), f32) for w in range(slots)]
    for t in range(15):
        o = one_rows[pl.ds(t, turns, stride=15), :]
        for w in range(slots):
            part_sum[w] = part_sum[w] + panel_rows[w, :turns, t * LANES : (t + 1) * LANES] * o
    one_part = jnp.concatenate(
        [jnp.sum(p, axis=0, keepdims=True) for p in part_sum], axis=0
    )
    one_part = jnp.sum(one_part, axis=1, keepdims=True)
    for w in range(slots):
        for q in range(16):
            theta_rows[pl.ds(w * ORB + q, turns, stride=16), :] = (
                panel_rows[w, :turns, q * ELEC : q * ELEC + LANES]
            )
    for w in range(slots):
        theta[:ORB, w * LANES : (w + 1) * LANES] = (
            theta_rows[w * ORB : (w + 1) * ORB, :].astype(bf16)
        )

    eye = (
        lax.broadcasted_iota(jnp.int32, (ELEC, ELEC), 0)
        == lax.broadcasted_iota(jnp.int32, (ELEC, ELEC), 1)
    )

    def terms(ref, carry):
        def multiply(g, c):
            block = pl.ds(pl.multiple_of(g * (2 * ELEC), 16), 2 * ELEC)
            f = jnp.dot(ref[block, :], theta[...], preferred_element_type=f32)
            for w in range(slots):
                products[w, block, :] = f[:, w * LANES : (w + 1) * LANES]
            return c

        lax.fori_loop(0, nchol // 2, multiply, 0)
        result = []
        for w in range(slots):
            square, cross = carry[w]
            for g in range(nchol):
                f = products.at[w][pl.ds(g, ELEC, stride=nchol), :][:, :ELEC]
                tr = jnp.sum(jnp.where(eye, f, 0.0), keepdims=True)
                square, cross = square + tr * tr, cross + f * f.T
            result.append((square, cross))
        return tuple(result)

    carry = tuple(
        (jnp.zeros((1, 1), f32), jnp.zeros((ELEC, ELEC), f32)) for _ in range(slots)
    )

    def announce(carry):
        for o in range(1, groups):
            chol_copies[o - 1].wait_recv()
            carry = terms(other.at[o - 1], carry)

        lane = lax.broadcasted_iota(jnp.int32, (1, LANES), 1)
        energy = jnp.zeros((1, LANES), f32)
        weights = jnp.zeros((1, LANES), f32)
        for w in range(slots):
            square, cross = carry[w]
            two_body = 0.5 * square - 0.5 * jnp.sum(cross, keepdims=True)
            energy = jnp.where(lane == w, one_part[w : w + 1] + two_body / ELEC, energy)
            weights = jnp.where(lane == w, weight_ref[w], weights)
        alive = (lane < count_ref[0]) & (lane < slots)
        sub = lax.broadcasted_iota(jnp.int32, (8, LANES), 0)
        messages[me] = jnp.where(
            sub == 0, energy, jnp.where((sub == 1) & alive, weights, 0.0)
        )

        def tell(d, c):
            j = (me + d) % n
            pltpu.make_async_remote_copy(
                src_ref=messages.at[me], dst_ref=messages.at[me],
                send_sem=sw, recv_sem=rw, device_id=at(j), device_id_type=mesh_ids,
            ).start()
            return c

        lax.fori_loop(1, n, tell, 0)

    leave(1)
    leave(2)
    deliver(0)
    carry = terms(slab, carry)
    leave(3)
    deliver(1)
    announce(carry)
    deliver(2)
    most = jnp.zeros((8, LANES), jnp.int32)
    if votes:
        most = counted[...]
        for o in range(1, parts):
            votes[o - 1].wait()
            most = jnp.maximum(most, told[o - 1])
    flag_ref[0] = (jnp.max(most) > room).astype(jnp.int32)
    flag_copy = pltpu.make_async_copy(flag_ref, flag_hbm, out)
    flag_copy.start()
    deliver(3)

    heard = messages.at[pl.ds(0, n - 1)]
    pltpu.make_async_copy(heard, heard, rw).wait()
    for k in range(STEPS):
        bulk = spread[k].at[pl.ds(0, half - 1)]
        pltpu.make_async_copy(bulk, bulk, r3.at[k]).wait()
        pltpu.make_async_copy(bulk, bulk, s1.at[k]).wait()
        pltpu.make_async_copy(cross[k], cross[k], s2.at[k]).wait()
        pltpu.make_async_copy(bulk, bulk, s3.at[k]).wait()

    for copy in chol_copies:
        copy.wait_send()
    pltpu.make_async_copy(heard, heard, sw).wait()
    flag_copy.wait()


CHUNKS = 1


def finish(
    panel_ref, messages, copy_ref, median_ref, clip_ref,
    energy_hbm, estimate_hbm, fresh_hbm, out_ref,
    energy_ref, estimate_ref, fresh_ref, sems,
):
    n, slots = messages.shape[0], out_ref.shape[0]
    me = lax.axis_index("walk") * lax.axis_size("chol") + lax.axis_index("chol")
    f32 = jnp.float32
    tiles = out_ref.shape[1] // LANES
    copies = []
    for i in range(CHUNKS):
        first, end = tiles * i // CHUNKS, tiles * (i + 1) // CHUNKS
        chunk = pl.ds(first * LANES, (end - first) * LANES)
        copy = pltpu.make_async_copy(
            panel_ref.at[:, chunk], out_ref.at[:, chunk], sems.at[i]
        )
        copy.start()
        copies.append(copy)
    lane = lax.broadcasted_iota(jnp.int32, (1, LANES), 1)
    energy, live = messages[:, 0, :], messages[:, 1, :]
    for w in range(slots):
        energy_ref[w] = jnp.sum(jnp.where(lane == w, messages[me][0:1], 0.0))
    wanted = copy_ref[...].reshape(1, -1)
    slot = lax.broadcasted_iota(jnp.int32, wanted.shape, 1)
    sources = [
        jnp.sum(jnp.where(slot == me * slots + w, wanted, 0), axis=1, keepdims=True)
        for w in range(slots)
    ]
    half_width = jnp.broadcast_to(clip_ref[...].reshape(1, 1), (n, LANES)).astype(f32) / 256.0
    median = jnp.broadcast_to(median_ref[...].reshape(1, 1), (n, LANES))
    clipped = jnp.minimum(jnp.maximum(energy, median - half_width), median + half_width)
    grown = jnp.where(live > 0.0, live * jnp.exp(-tau_step * (clipped - median)), 0.0)
    place = lax.broadcasted_iota(jnp.int32, (n, LANES), 0) * slots
    column = lax.broadcasted_iota(jnp.int32, (n, LANES), 1)
    place = jnp.where(column < slots, place + column, -1)
    weight_sum = jnp.sum(grown, keepdims=True)
    weighted = jnp.sum(grown * clipped, keepdims=True)
    copied = [
        jnp.sum(jnp.where(place == source, grown, 0.0), keepdims=True) for source in sources
    ]
    scale = (n * slots) / weight_sum
    estimate_ref[0] = (weighted / weight_sum)[0, 0]
    for w in range(slots):
        fresh_ref[w] = (copied[w] * scale)[0, 0]
    results = [
        pltpu.make_async_copy(source, target, sems.at[CHUNKS + i])
        for i, (source, target) in enumerate((
            (energy_ref, energy_hbm), (estimate_ref, estimate_hbm), (fresh_ref, fresh_hbm),
        ))
    ]
    for copy in results:
        copy.start()
    for copy in copies + results:
        copy.wait()


def per_device(green, chol_vecs, one_body, weights, counts, copy_list, e_median, clip_bin):
    slots, length = green.shape
    nchol = chol_vecs.shape[0]
    groups = lax.axis_size("chol")
    n = lax.axis_size("walk") * groups
    parts = lax.axis_size("ens")
    tiles = length // LANES
    units = n // 2 * STEPS
    unit = -(-tiles // units)
    width = unit * LANES
    half = n // 2
    deep = -(-ORB // 256) * 256
    wide = max(units * unit, tiles + 1) * LANES
    bf16, f32 = jnp.bfloat16, jnp.float32
    vmem = pl.BlockSpec(memory_space=pltpu.VMEM)
    smem = pl.BlockSpec(memory_space=pltpu.SMEM)
    hbm = pl.BlockSpec(memory_space=pltpu.HBM)
    dma = pltpu.SemaphoreType.DMA

    operands = (
        copy_list, weights, counts,
        green, chol_vecs, one_body.reshape(tiles, LANES),
    )
    def run(room, number, *operands):
        def buffer(rows):
            return [pltpu.VMEM((rows, slots, width), bf16)] * STEPS

        spare = [pltpu.VMEM((1, slots, LANES), bf16)] * STEPS
        return pl.pallas_call(
            functools.partial(body, n, groups, unit, room),
            out_shape=(
                jax.ShapeDtypeStruct((slots, wide), bf16),
                jax.ShapeDtypeStruct((n, 8, LANES), f32),
                jax.ShapeDtypeStruct((1,), jnp.int32),
            ),
            in_specs=[hbm] * 6,
            out_specs=(vmem, vmem, hbm),
            scratch_shapes=[
                    pltpu.VMEM((slots, wide), bf16),
                    pltpu.VMEM((nchol * ELEC, deep), bf16),
                    pltpu.VMEM((groups - 1, nchol * ELEC, deep), bf16),
                    pltpu.VMEM((slots, -(-(ORB // 16) // 8) * 8, 16 * LANES), f32),
                    pltpu.VMEM((slots * ORB, LANES), f32),
                    pltpu.VMEM((deep, slots * LANES), bf16),
                    pltpu.VMEM((nchol * ELEC, deep), f32),
                    pltpu.VMEM((slots, nchol * ELEC, LANES), f32),
                    pltpu.VMEM((tiles, LANES), f32),
                    pltpu.VMEM(chol_vecs.shape, bf16),
                    pltpu.VMEM((tiles, LANES), bf16),
                    pltpu.SMEM(copy_list.shape, jnp.int32),
                    pltpu.SMEM(weights.shape, f32),
                    pltpu.SMEM((1,), jnp.int32),
                    pltpu.SMEM((half * slots,), jnp.int32),
                    pltpu.SMEM((room,), jnp.int32),
                    pltpu.VMEM((8, LANES), jnp.int32),
                    pltpu.VMEM((parts - 1, 8, LANES), jnp.int32),
                    pltpu.SMEM((1,), jnp.int32),
                    dma((STEPS,)), dma((8,)), dma((parts - 1,)), dma((parts - 1,)), dma,
                    *[dma((STEPS,))] * 6,
                    dma((groups - 1,)), dma((groups - 1,)), dma, dma,
                    *buffer(half), *buffer(room // slots),
                    *(buffer(room // slots) if room < half * slots else spare),
                    *buffer(half),
            ],
            compiler_params=pltpu.CompilerParams(
                collective_id=number, has_side_effects=True,
                vmem_limit_bytes=60 * 1024 * 1024,
            ),
        )(*operands)

    def hand_over(panels, messages):
        return pl.pallas_call(
            finish,
            out_shape=(
                jax.ShapeDtypeStruct((slots,), f32),
                jax.ShapeDtypeStruct((1,), f32),
                jax.ShapeDtypeStruct((slots,), f32),
                jax.ShapeDtypeStruct((slots, length), bf16),
            ),
            in_specs=[vmem] * 5,
            out_specs=(hbm,) * 4,
            scratch_shapes=[
                pltpu.SMEM((slots,), f32),
                pltpu.SMEM((1,), f32),
                pltpu.SMEM((slots,), f32),
                dma((CHUNKS + 3,)),
            ],
        )(panels, messages, copy_list, e_median, clip_bin)

    panels, messages, flag = run(min(ROOM, half * slots), 0, *operands)
    return lax.switch(
        flag[0],
        (
            lambda panels, messages, *operands: hand_over(panels, messages),
            lambda panels, messages, *operands: hand_over(
                *run(half * slots, 1, *operands)[:2]
            ),
        ),
        panels, messages, *operands,
    )


def solution(mesh):
    placed = (
        P(("ens", "walk", "chol"), None),
        P("chol", None),
        P(),
        P(("ens", "walk", "chol")),
        P(("ens", "walk", "chol")),
        P("ens"),
        P("ens"),
        P("ens"),
    )
    return jax.shard_map(
        per_device,
        mesh=mesh,
        in_specs=placed,
        out_specs=(
            P(("ens", "walk", "chol")),
            P("ens"),
            P(("ens", "walk", "chol")),
            P(("ens", "walk", "chol"), None),
        ),
        check_vma=False,
    )
```

```python
import functools

import jax
import jax.numpy as jnp
from jax import lax
from jax.experimental import pallas as pl
from jax.experimental.pallas import tpu as pltpu
from jax.sharding import PartitionSpec as P

ORB = 1200
ELEC = 120
LANES = 128
STEPS = 4
LINE = 2
ROOM = 8


tau_step = 0.2


def body(
    n, groups, unit, room,
    copy_hbm, weight_hbm, count_hbm,
    panel_ref, chol_hbm, one_hbm,
    landed, messages, flag_hbm,
    padded, slab, other,
    panel_rows, theta_rows, theta, slab_rows, products, one_rows,
    chol_ref, one_ref, copy_ref, weight_ref, count_ref,
    table, asked, counted, told, flag_ref,
    lp, local, sv, rv, out, s1, r1, s2, r2, s3, r3, sc, rc, sw, rw,
    *buffers,
):
    slots, length = panel_ref.shape
    nchol = chol_ref.shape[0]
    half = n // 2
    width = unit * LANES
    spread, cross, leaving, picked = [
        buffers[i * STEPS : (i + 1) * STEPS] for i in range(4)
    ]
    everything = room >= half * slots
    chol_index = lax.axis_index("chol")
    me = lax.axis_index("walk") * groups + chol_index
    side, here = lax.div(me, half), lax.rem(me, half)
    parts, part = lax.axis_size("ens"), lax.axis_index("ens")
    mesh_ids = pl.DeviceIdType.MESH
    f32, bf16 = jnp.float32, jnp.bfloat16

    def at(j):
        return {"walk": lax.div(j, groups), "chol": lax.rem(j, groups)}

    def mirror(h):
        return half - LINE * groups * (1 + lax.div(h, LINE * groups)) + lax.rem(h, LINE * groups)

    across = mirror(here)

    def place(h, k):
        h = jnp.where(side == 0, h, mirror(h))
        return pl.ds(pl.multiple_of((k * half + h) * width, LANES), width)

    barrier = pltpu.get_barrier_semaphore()
    panel_fetches = []
    for k in range(STEPS):
        first = min(k * half * width, length)
        part_of = pl.ds(first, min((k + 1) * half * width, length) - first)
        if first < length:
            fetch = pltpu.make_async_copy(
                panel_ref.at[:, part_of], padded.at[:, part_of], lp.at[k]
            )
            fetch.start()
            panel_fetches.append(fetch)

    def greet(d, c):
        pl.semaphore_signal(
            barrier, inc=1, device_id=at(lax.rem(me + d, n)), device_id_type=mesh_ids
        )
        return c

    lax.fori_loop(1, n, greet, 0)
    for o in range(1, parts):
        pl.semaphore_signal(
            barrier, inc=1, device_id={"ens": (part + o) % parts}, device_id_type=mesh_ids
        )
    fetches = [
        pltpu.make_async_copy(source, target, local.at[1 + i])
        for i, (source, target) in enumerate((
            (chol_hbm, chol_ref), (one_hbm, one_ref), (copy_hbm, copy_ref),
            (weight_hbm, weight_ref), (count_hbm, count_ref),
        ))
    ]
    padded[:, length:] = jnp.zeros((slots, padded.shape[1] - length), bf16)
    pl.semaphore_wait(barrier, n - 1 + parts - 1)

    for k in range(STEPS):
        for fetch in panel_fetches[k : k + 1]:
            fetch.wait()

        def send_slice(d, c):
            h = lax.rem(here + d, half)
            pltpu.make_async_remote_copy(
                src_ref=padded.at[:, place(h, k)], dst_ref=spread[k].at[here],
                send_sem=s1.at[k], recv_sem=r1.at[k],
                device_id=at(side * half + h), device_id_type=mesh_ids,
            ).start()
            return c

        lax.fori_loop(1, half, send_slice, 0)
    for copy in fetches:
        copy.start()
    for k in range(STEPS):
        spread[k][here] = padded[:, place(here, k)]
    for copy in fetches:
        copy.wait()

    split = half * slots
    base, away = side * split, (1 - side) * split

    def read_own(d, carry):
        before, rank = carry
        source = copy_ref[base + d]
        comes = source // split != side
        fresh = comes & (source != before)
        rank = rank + fresh.astype(jnp.int32)
        place = source - away if everything else jnp.minimum(rank - 1, room - 1)
        table[d] = jnp.where(comes, split + place, source - base)
        return source, rank

    arriving = lax.fori_loop(0, split, read_own, (jnp.int32(-1), jnp.int32(0)))[1]
    votes = []
    if not everything:

        def read_away(d, carry):
            before, rank, chosen = carry
            source = copy_ref[away + d]
            fresh = (source // split == side) & (source != before)
            chosen = tuple(
                jnp.where(fresh & (rank == m), source - base, chosen[m])
                for m in range(room)
            )
            return source, rank + fresh.astype(jnp.int32), chosen

        _, departing, chosen = lax.fori_loop(
            0, split, read_away,
            (jnp.int32(-1), jnp.int32(0), (jnp.int32(0),) * room),
        )
        for m in range(room):
            asked[m] = chosen[m]
        counted[...] = jnp.full(counted.shape, jnp.maximum(arriving, departing), jnp.int32)
        for o in range(1, parts):
            vote = pltpu.make_async_remote_copy(
                src_ref=counted, dst_ref=told.at[o - 1],
                send_sem=sv.at[o - 1], recv_sem=rv.at[o - 1],
                device_id={"ens": (part + o) % parts}, device_id_type=mesh_ids,
            )
            vote.start()
            votes.append(vote)

    step = 8 * LANES
    pieces = [(f, min(step, width - f)) for f in range(0, width, step)]

    def merge(lines_of, size):
        spot = lax.broadcasted_iota(jnp.int32, (slots, size), 0)
        value = None
        for k, (x, row) in enumerate(lines_of):
            picked_line = x[0:1]
            for w in range(1, slots):
                picked_line = jnp.where(row == w, x[w : w + 1], picked_line)
            picked_line = jnp.broadcast_to(picked_line, (slots, size))
            value = picked_line if value is None else jnp.where(spot == k, picked_line, value)
        return value.astype(bf16)

    def leave(k):
        bulk = spread[k].at[pl.ds(0, half - 1)]
        pltpu.make_async_copy(bulk, bulk, r1.at[k]).wait()
        source = spread[k]
        if not everything:
            source = leaving[k]

            def gather(j, c):
                sources = [asked[j * slots + i] for i in range(slots)]
                for first, size in pieces:
                    leaving[k][j, :, first : first + size] = merge(
                        [
                            (spread[k][p // slots, :, first : first + size].astype(f32), p % slots)
                            for p in sources
                        ],
                        size,
                    )
                return c

            lax.fori_loop(0, room // slots, gather, 0)
        pltpu.make_async_remote_copy(
            src_ref=source, dst_ref=cross[k],
            send_sem=s2.at[k], recv_sem=r2.at[k],
            device_id=at((1 - side) * half + across), device_id_type=mesh_ids,
        ).start()

    def deliver(k):
        pltpu.make_async_copy(cross[k], cross[k], r2.at[k]).wait()
        to = place(here, k)

        def pick(j):
            sources = [table[j * slots + i] for i in range(slots)]
            for first, size in pieces:
                found = []
                for p in sources:
                    comes = p >= split
                    a = jnp.where(comes, 0, p)
                    b = jnp.where(comes, p - split, 0)
                    x = spread[k][a // slots, :, first : first + size].astype(f32)
                    y = cross[k][b // slots, :, first : first + size].astype(f32)
                    found.append((jnp.where(comes, y, x), p % slots))
                picked[k][j, :, first : first + size] = merge(found, size)

        def send_back(d, c):
            j = lax.rem(here + d, half)
            pick(j)
            pltpu.make_async_remote_copy(
                src_ref=picked[k].at[j], dst_ref=landed.at[:, to],
                send_sem=s3.at[k], recv_sem=r3.at[k],
                device_id=at(side * half + j), device_id_type=mesh_ids,
            ).start()
            return c

        lax.fori_loop(1, half, send_back, 0)
        pick(here)
        landed[:, to] = picked[k][here]

    deep = slab.shape[1]
    slab_rows[:, ORB:] = jnp.zeros((slab_rows.shape[0], deep - ORB), f32)

    def chol_step(r, c):
        x = chol_ref[:, pl.ds(pl.multiple_of(r * (8 * ORB), LANES), 8 * ORB)].astype(f32)
        block = pl.ds(pl.multiple_of(r * (8 * nchol), 8), 8 * nchol)
        slab_rows[block, :ORB] = jnp.concatenate(
            [x[:, k * ORB : (k + 1) * ORB] for k in range(8)], axis=0
        )
        return c

    lax.fori_loop(0, ELEC // 8, chol_step, 0, unroll=3)
    slab[...] = slab_rows[...].astype(bf16)
    chol_copies = []
    for o in range(1, groups):
        copy = pltpu.make_async_remote_copy(
            src_ref=slab, dst_ref=other.at[o - 1],
            send_sem=sc.at[o - 1], recv_sem=rc.at[o - 1],
            device_id={"chol": (chol_index + o) % groups}, device_id_type=mesh_ids,
        )
        copy.start()
        chol_copies.append(copy)


    leave(0)
    eye = (
        lax.broadcasted_iota(jnp.int32, (ELEC, ELEC), 0)
        == lax.broadcasted_iota(jnp.int32, (ELEC, ELEC), 1)
    )

    def terms(ref, carry):
        def multiply(g, c):
            block = pl.ds(pl.multiple_of(g * (2 * ELEC), 16), 2 * ELEC)
            f = jnp.dot(ref[block, :], theta[...], preferred_element_type=f32)
            for w in range(slots):
                products[w, block, :] = f[:, w * LANES : (w + 1) * LANES]
            return c

        lax.fori_loop(0, nchol // 2, multiply, 0)
        result = []
        for w in range(slots):
            square, cross = carry[w]
            for g in range(nchol):
                f = products.at[w][pl.ds(g, ELEC, stride=nchol), :][:, :ELEC]
                tr = jnp.sum(jnp.where(eye, f, 0.0), keepdims=True)
                square, cross = square + tr * tr, cross + f * f.T
            result.append((square, cross))
        return tuple(result)

    carry = tuple(
        (jnp.zeros((1, 1), f32), jnp.zeros((ELEC, ELEC), f32)) for _ in range(slots)
    )

    def announce(carry):
        for o in range(1, groups):
            chol_copies[o - 1].wait_recv()
            carry = terms(other.at[o - 1], carry)

        lane = lax.broadcasted_iota(jnp.int32, (1, LANES), 1)
        energy = jnp.zeros((1, LANES), f32)
        weights = jnp.zeros((1, LANES), f32)
        for w in range(slots):
            square, cross = carry[w]
            two_body = 0.5 * square - 0.5 * jnp.sum(cross, keepdims=True)
            energy = jnp.where(lane == w, one_part[w : w + 1] + two_body / ELEC, energy)
            weights = jnp.where(lane == w, weight_ref[w], weights)
        alive = (lane < count_ref[0]) & (lane < slots)
        sub = lax.broadcasted_iota(jnp.int32, (8, LANES), 0)
        messages[me] = jnp.where(
            sub == 0, energy, jnp.where((sub == 1) & alive, weights, 0.0)
        )

        def tell(d, c):
            j = (me + d) % n
            pltpu.make_async_remote_copy(
                src_ref=messages.at[me], dst_ref=messages.at[me],
                send_sem=sw, recv_sem=rw, device_id=at(j), device_id_type=mesh_ids,
            ).start()
            return c

        lax.fori_loop(1, n, tell, 0)

    leave(1)
    one_rows[...] = one_ref[...].astype(f32)
    theta[ORB:] = jnp.zeros((deep - ORB, slots * LANES), bf16)

    def rows_step(r, c):
        x = padded[:, pl.ds(pl.multiple_of(r * (16 * ELEC), LANES), 16 * LANES)].astype(f32)
        for w in range(slots):
            panel_rows[w, pl.ds(r, 1), :] = x[w : w + 1]
        return c

    turns = ORB // 16
    lax.fori_loop(0, turns, rows_step, 0, unroll=5)
    part_sum = [jnp.zeros((turns, LANES), f32) for w in range(slots)]
    for t in range(15):
        o = one_rows[pl.ds(t, turns, stride=15), :]
        for w in range(slots):
            part_sum[w] = part_sum[w] + panel_rows[w, :turns, t * LANES : (t + 1) * LANES] * o
    one_part = jnp.concatenate(
        [jnp.sum(p, axis=0, keepdims=True) for p in part_sum], axis=0
    )
    one_part = jnp.sum(one_part, axis=1, keepdims=True)
    for w in range(slots):
        for q in range(16):
            theta_rows[pl.ds(w * ORB + q, turns, stride=16), :] = (
                panel_rows[w, :turns, q * ELEC : q * ELEC + LANES]
            )
    for w in range(slots):
        theta[:ORB, w * LANES : (w + 1) * LANES] = (
            theta_rows[w * ORB : (w + 1) * ORB, :].astype(bf16)
        )

    leave(2)
    deliver(0)
    carry = terms(slab, carry)
    leave(3)
    deliver(1)
    announce(carry)
    deliver(2)
    most = jnp.zeros((8, LANES), jnp.int32)
    if votes:
        most = counted[...]
        for o in range(1, parts):
            votes[o - 1].wait()
            most = jnp.maximum(most, told[o - 1])
    flag_ref[0] = (jnp.max(most) > room).astype(jnp.int32)
    flag_copy = pltpu.make_async_copy(flag_ref, flag_hbm, out)
    flag_copy.start()
    deliver(3)

    heard = messages.at[pl.ds(0, n - 1)]
    pltpu.make_async_copy(heard, heard, rw).wait()
    for k in range(STEPS):
        bulk = spread[k].at[pl.ds(0, half - 1)]
        pltpu.make_async_copy(bulk, bulk, r3.at[k]).wait()
        pltpu.make_async_copy(bulk, bulk, s1.at[k]).wait()
        pltpu.make_async_copy(cross[k], cross[k], s2.at[k]).wait()
        pltpu.make_async_copy(bulk, bulk, s3.at[k]).wait()

    for copy in chol_copies:
        copy.wait_send()
    pltpu.make_async_copy(heard, heard, sw).wait()
    flag_copy.wait()


CHUNKS = 1


def finish(
    panel_ref, messages, copy_ref, median_ref, clip_ref,
    energy_hbm, estimate_hbm, fresh_hbm, out_ref,
    energy_ref, estimate_ref, fresh_ref, sems,
):
    n, slots = messages.shape[0], out_ref.shape[0]
    me = lax.axis_index("walk") * lax.axis_size("chol") + lax.axis_index("chol")
    f32 = jnp.float32
    tiles = out_ref.shape[1] // LANES
    copies = []
    for i in range(CHUNKS):
        first, end = tiles * i // CHUNKS, tiles * (i + 1) // CHUNKS
        chunk = pl.ds(first * LANES, (end - first) * LANES)
        copy = pltpu.make_async_copy(
            panel_ref.at[:, chunk], out_ref.at[:, chunk], sems.at[i]
        )
        copy.start()
        copies.append(copy)
    lane = lax.broadcasted_iota(jnp.int32, (1, LANES), 1)
    energy, live = messages[:, 0, :], messages[:, 1, :]
    for w in range(slots):
        energy_ref[w] = jnp.sum(jnp.where(lane == w, messages[me][0:1], 0.0))
    wanted = copy_ref[...].reshape(1, -1)
    slot = lax.broadcasted_iota(jnp.int32, wanted.shape, 1)
    sources = [
        jnp.sum(jnp.where(slot == me * slots + w, wanted, 0), axis=1, keepdims=True)
        for w in range(slots)
    ]
    half_width = jnp.broadcast_to(clip_ref[...].reshape(1, 1), (n, LANES)).astype(f32) / 256.0
    median = jnp.broadcast_to(median_ref[...].reshape(1, 1), (n, LANES))
    clipped = jnp.minimum(jnp.maximum(energy, median - half_width), median + half_width)
    grown = jnp.where(live > 0.0, live * jnp.exp(-tau_step * (clipped - median)), 0.0)
    place = lax.broadcasted_iota(jnp.int32, (n, LANES), 0) * slots
    column = lax.broadcasted_iota(jnp.int32, (n, LANES), 1)
    place = jnp.where(column < slots, place + column, -1)
    weight_sum = jnp.sum(grown, keepdims=True)
    weighted = jnp.sum(grown * clipped, keepdims=True)
    copied = [
        jnp.sum(jnp.where(place == source, grown, 0.0), keepdims=True) for source in sources
    ]
    scale = (n * slots) / weight_sum
    estimate_ref[0] = (weighted / weight_sum)[0, 0]
    for w in range(slots):
        fresh_ref[w] = (copied[w] * scale)[0, 0]
    results = [
        pltpu.make_async_copy(source, target, sems.at[CHUNKS + i])
        for i, (source, target) in enumerate((
            (energy_ref, energy_hbm), (estimate_ref, estimate_hbm), (fresh_ref, fresh_hbm),
        ))
    ]
    for copy in results:
        copy.start()
    for copy in copies + results:
        copy.wait()


def per_device(green, chol_vecs, one_body, weights, counts, copy_list, e_median, clip_bin):
    slots, length = green.shape
    nchol = chol_vecs.shape[0]
    groups = lax.axis_size("chol")
    n = lax.axis_size("walk") * groups
    parts = lax.axis_size("ens")
    tiles = length // LANES
    units = n // 2 * STEPS
    unit = -(-tiles // units)
    width = unit * LANES
    half = n // 2
    deep = -(-ORB // 256) * 256
    wide = max(units * unit, tiles + 1) * LANES
    bf16, f32 = jnp.bfloat16, jnp.float32
    vmem = pl.BlockSpec(memory_space=pltpu.VMEM)
    smem = pl.BlockSpec(memory_space=pltpu.SMEM)
    hbm = pl.BlockSpec(memory_space=pltpu.HBM)
    dma = pltpu.SemaphoreType.DMA

    operands = (
        copy_list, weights, counts,
        green, chol_vecs, one_body.reshape(tiles, LANES),
    )
    def run(room, number, *operands):
        def buffer(rows):
            return [pltpu.VMEM((rows, slots, width), bf16)] * STEPS

        spare = [pltpu.VMEM((1, slots, LANES), bf16)] * STEPS
        return pl.pallas_call(
            functools.partial(body, n, groups, unit, room),
            out_shape=(
                jax.ShapeDtypeStruct((slots, wide), bf16),
                jax.ShapeDtypeStruct((n, 8, LANES), f32),
                jax.ShapeDtypeStruct((1,), jnp.int32),
            ),
            in_specs=[hbm] * 6,
            out_specs=(vmem, vmem, hbm),
            scratch_shapes=[
                    pltpu.VMEM((slots, wide), bf16),
                    pltpu.VMEM((nchol * ELEC, deep), bf16),
                    pltpu.VMEM((groups - 1, nchol * ELEC, deep), bf16),
                    pltpu.VMEM((slots, -(-(ORB // 16) // 8) * 8, 16 * LANES), f32),
                    pltpu.VMEM((slots * ORB, LANES), f32),
                    pltpu.VMEM((deep, slots * LANES), bf16),
                    pltpu.VMEM((nchol * ELEC, deep), f32),
                    pltpu.VMEM((slots, nchol * ELEC, LANES), f32),
                    pltpu.VMEM((tiles, LANES), f32),
                    pltpu.VMEM(chol_vecs.shape, bf16),
                    pltpu.VMEM((tiles, LANES), bf16),
                    pltpu.SMEM(copy_list.shape, jnp.int32),
                    pltpu.SMEM(weights.shape, f32),
                    pltpu.SMEM((1,), jnp.int32),
                    pltpu.SMEM((half * slots,), jnp.int32),
                    pltpu.SMEM((room,), jnp.int32),
                    pltpu.VMEM((8, LANES), jnp.int32),
                    pltpu.VMEM((parts - 1, 8, LANES), jnp.int32),
                    pltpu.SMEM((1,), jnp.int32),
                    dma((STEPS,)), dma((8,)), dma((parts - 1,)), dma((parts - 1,)), dma,
                    *[dma((STEPS,))] * 6,
                    dma((groups - 1,)), dma((groups - 1,)), dma, dma,
                    *buffer(half), *buffer(room // slots),
                    *(buffer(room // slots) if room < half * slots else spare),
                    *buffer(half),
            ],
            compiler_params=pltpu.CompilerParams(
                collective_id=number, has_side_effects=True,
                vmem_limit_bytes=60 * 1024 * 1024,
            ),
        )(*operands)

    def hand_over(panels, messages):
        return pl.pallas_call(
            finish,
            out_shape=(
                jax.ShapeDtypeStruct((slots,), f32),
                jax.ShapeDtypeStruct((1,), f32),
                jax.ShapeDtypeStruct((slots,), f32),
                jax.ShapeDtypeStruct((slots, length), bf16),
            ),
            in_specs=[vmem] * 5,
            out_specs=(hbm,) * 4,
            scratch_shapes=[
                pltpu.SMEM((slots,), f32),
                pltpu.SMEM((1,), f32),
                pltpu.SMEM((slots,), f32),
                dma((CHUNKS + 3,)),
            ],
        )(panels, messages, copy_list, e_median, clip_bin)

    panels, messages, flag = run(min(ROOM, half * slots), 0, *operands)
    return lax.switch(
        flag[0],
        (
            lambda panels, messages, *operands: hand_over(panels, messages),
            lambda panels, messages, *operands: hand_over(
                *run(half * slots, 1, *operands)[:2]
            ),
        ),
        panels, messages, *operands,
    )


def solution(mesh):
    placed = (
        P(("ens", "walk", "chol"), None),
        P("chol", None),
        P(),
        P(("ens", "walk", "chol")),
        P(("ens", "walk", "chol")),
        P("ens"),
        P("ens"),
        P("ens"),
    )
    return jax.shard_map(
        per_device,
        mesh=mesh,
        in_specs=placed,
        out_specs=(
            P(("ens", "walk", "chol")),
            P("ens"),
            P(("ens", "walk", "chol")),
            P(("ens", "walk", "chol"), None),
        ),
        check_vma=False,
    )
```

```python
import functools

import jax
import jax.numpy as jnp
from jax import lax
from jax.experimental import pallas as pl
from jax.experimental.pallas import tpu as pltpu
from jax.sharding import PartitionSpec as P

ORB = 1200
ELEC = 120
LANES = 128
STEPS = 4
LINE = 2
ROOM = 8


tau_step = 0.2


def body(
    n, groups, unit, room,
    copy_hbm, weight_hbm, count_hbm,
    panel_ref, chol_hbm, one_hbm,
    landed, messages, flag_hbm,
    padded, slab, other,
    panel_rows, theta_rows, theta, slab_rows, products, one_rows,
    chol_ref, one_ref, copy_ref, weight_ref, count_ref,
    table, asked, counted, told, flag_ref,
    lp, local, sv, rv, out, s1, r1, s2, r2, s3, r3, sc, rc, sw, rw,
    *buffers,
):
    slots, length = panel_ref.shape
    nchol = chol_ref.shape[0]
    half = n // 2
    width = unit * LANES
    spread, cross, leaving, picked = [
        buffers[i * STEPS : (i + 1) * STEPS] for i in range(4)
    ]
    everything = room >= half * slots
    chol_index = lax.axis_index("chol")
    me = lax.axis_index("walk") * groups + chol_index
    side, here = lax.div(me, half), lax.rem(me, half)
    parts, part = lax.axis_size("ens"), lax.axis_index("ens")
    mesh_ids = pl.DeviceIdType.MESH
    f32, bf16 = jnp.float32, jnp.bfloat16

    def at(j):
        return {"walk": lax.div(j, groups), "chol": lax.rem(j, groups)}

    def mirror(h):
        return half - LINE * groups * (1 + lax.div(h, LINE * groups)) + lax.rem(h, LINE * groups)

    across = mirror(here)

    def place(h, k):
        h = jnp.where(side == 0, h, mirror(h))
        return pl.ds(pl.multiple_of((k * half + h) * width, LANES), width)

    barrier = pltpu.get_barrier_semaphore()
    panel_fetches = []
    for k in range(STEPS):
        first = min(k * half * width, length)
        part_of = pl.ds(first, min((k + 1) * half * width, length) - first)
        if first < length:
            fetch = pltpu.make_async_copy(
                panel_ref.at[:, part_of], padded.at[:, part_of], lp.at[k]
            )
            fetch.start()
            panel_fetches.append(fetch)

    def greet(d, c):
        pl.semaphore_signal(
            barrier, inc=1, device_id=at(lax.rem(me + d, n)), device_id_type=mesh_ids
        )
        return c

    lax.fori_loop(1, n, greet, 0)
    for o in range(1, parts):
        pl.semaphore_signal(
            barrier, inc=1, device_id={"ens": (part + o) % parts}, device_id_type=mesh_ids
        )
    fetches = [
        pltpu.make_async_copy(source, target, local.at[1 + i])
        for i, (source, target) in enumerate((
            (chol_hbm, chol_ref), (one_hbm, one_ref), (copy_hbm, copy_ref),
            (weight_hbm, weight_ref), (count_hbm, count_ref),
        ))
    ]
    for copy in fetches:
        copy.start()
    padded[:, length:] = jnp.zeros((slots, padded.shape[1] - length), bf16)
    pl.semaphore_wait(barrier, n - 1 + parts - 1)

    for k in range(STEPS):
        for fetch in panel_fetches[k : k + 1]:
            fetch.wait()

        def send_slice(d, c):
            h = lax.rem(here + d, half)
            pltpu.make_async_remote_copy(
                src_ref=padded.at[:, place(h, k)], dst_ref=spread[k].at[here],
                send_sem=s1.at[k], recv_sem=r1.at[k],
                device_id=at(side * half + h), device_id_type=mesh_ids,
            ).start()
            return c

        lax.fori_loop(1, half, send_slice, 0)
    for k in range(STEPS):
        spread[k][here] = padded[:, place(here, k)]
    for copy in fetches:
        copy.wait()

    split = half * slots
    base, away = side * split, (1 - side) * split

    def read_own(d, carry):
        before, rank = carry
        source = copy_ref[base + d]
        comes = source // split != side
        fresh = comes & (source != before)
        rank = rank + fresh.astype(jnp.int32)
        place = source - away if everything else jnp.minimum(rank - 1, room - 1)
        table[d] = jnp.where(comes, split + place, source - base)
        return source, rank

    arriving = lax.fori_loop(0, split, read_own, (jnp.int32(-1), jnp.int32(0)))[1]
    votes = []
    if not everything:

        def read_away(d, carry):
            before, rank, chosen = carry
            source = copy_ref[away + d]
            fresh = (source // split == side) & (source != before)
            chosen = tuple(
                jnp.where(fresh & (rank == m), source - base, chosen[m])
                for m in range(room)
            )
            return source, rank + fresh.astype(jnp.int32), chosen

        _, departing, chosen = lax.fori_loop(
            0, split, read_away,
            (jnp.int32(-1), jnp.int32(0), (jnp.int32(0),) * room),
        )
        for m in range(room):
            asked[m] = chosen[m]
        counted[...] = jnp.full(counted.shape, jnp.maximum(arriving, departing), jnp.int32)
        for o in range(1, parts):
            vote = pltpu.make_async_remote_copy(
                src_ref=counted, dst_ref=told.at[o - 1],
                send_sem=sv.at[o - 1], recv_sem=rv.at[o - 1],
                device_id={"ens": (part + o) % parts}, device_id_type=mesh_ids,
            )
            vote.start()
            votes.append(vote)

    step = 8 * LANES
    pieces = [(f, min(step, width - f)) for f in range(0, width, step)]

    def merge(lines_of, size):
        spot = lax.broadcasted_iota(jnp.int32, (slots, size), 0)
        value = None
        for k, (x, row) in enumerate(lines_of):
            picked_line = x[0:1]
            for w in range(1, slots):
                picked_line = jnp.where(row == w, x[w : w + 1], picked_line)
            picked_line = jnp.broadcast_to(picked_line, (slots, size))
            value = picked_line if value is None else jnp.where(spot == k, picked_line, value)
        return value.astype(bf16)

    def leave(k):
        bulk = spread[k].at[pl.ds(0, half - 1)]
        pltpu.make_async_copy(bulk, bulk, r1.at[k]).wait()
        source = spread[k]
        if not everything:
            source = leaving[k]

            def gather(j, c):
                sources = [asked[j * slots + i] for i in range(slots)]
                for first, size in pieces:
                    leaving[k][j, :, first : first + size] = merge(
                        [
                            (spread[k][p // slots, :, first : first + size].astype(f32), p % slots)
                            for p in sources
                        ],
                        size,
                    )
                return c

            lax.fori_loop(0, room // slots, gather, 0)
        pltpu.make_async_remote_copy(
            src_ref=source, dst_ref=cross[k],
            send_sem=s2.at[k], recv_sem=r2.at[k],
            device_id=at((1 - side) * half + across), device_id_type=mesh_ids,
        ).start()

    def deliver(k):
        pltpu.make_async_copy(cross[k], cross[k], r2.at[k]).wait()
        to = place(here, k)

        def pick(j):
            sources = [table[j * slots + i] for i in range(slots)]
            for first, size in pieces:
                found = []
                for p in sources:
                    comes = p >= split
                    a = jnp.where(comes, 0, p)
                    b = jnp.where(comes, p - split, 0)
                    x = spread[k][a // slots, :, first : first + size].astype(f32)
                    y = cross[k][b // slots, :, first : first + size].astype(f32)
                    found.append((jnp.where(comes, y, x), p % slots))
                picked[k][j, :, first : first + size] = merge(found, size)

        def send_back(d, c):
            j = lax.rem(here + d, half)
            pick(j)
            pltpu.make_async_remote_copy(
                src_ref=picked[k].at[j], dst_ref=landed.at[:, to],
                send_sem=s3.at[k], recv_sem=r3.at[k],
                device_id=at(side * half + j), device_id_type=mesh_ids,
            ).start()
            return c

        lax.fori_loop(1, half, send_back, 0)
        pick(here)
        landed[:, to] = picked[k][here]

    deep = slab.shape[1]
    slab_rows[:, ORB:] = jnp.zeros((slab_rows.shape[0], deep - ORB), f32)

    def chol_step(r, c):
        x = chol_ref[:, pl.ds(pl.multiple_of(r * (8 * ORB), LANES), 8 * ORB)].astype(f32)
        block = pl.ds(pl.multiple_of(r * (8 * nchol), 8), 8 * nchol)
        slab_rows[block, :ORB] = jnp.concatenate(
            [x[:, k * ORB : (k + 1) * ORB] for k in range(8)], axis=0
        )
        return c

    lax.fori_loop(0, ELEC // 8, chol_step, 0, unroll=3)
    slab[...] = slab_rows[...].astype(bf16)
    chol_copies = []
    for o in range(1, groups):
        copy = pltpu.make_async_remote_copy(
            src_ref=slab, dst_ref=other.at[o - 1],
            send_sem=sc.at[o - 1], recv_sem=rc.at[o - 1],
            device_id={"chol": (chol_index + o) % groups}, device_id_type=mesh_ids,
        )
        copy.start()
        chol_copies.append(copy)


    leave(0)
    eye = (
        lax.broadcasted_iota(jnp.int32, (ELEC, ELEC), 0)
        == lax.broadcasted_iota(jnp.int32, (ELEC, ELEC), 1)
    )

    def terms(ref, carry):
        def multiply(g, c):
            block = pl.ds(pl.multiple_of(g * (2 * ELEC), 16), 2 * ELEC)
            f = jnp.dot(ref[block, :], theta[...], preferred_element_type=f32)
            for w in range(slots):
                products[w, block, :] = f[:, w * LANES : (w + 1) * LANES]
            return c

        lax.fori_loop(0, nchol // 2, multiply, 0)
        result = []
        for w in range(slots):
            square, cross = carry[w]
            for g in range(nchol):
                f = products.at[w][pl.ds(g, ELEC, stride=nchol), :][:, :ELEC]
                tr = jnp.sum(jnp.where(eye, f, 0.0), keepdims=True)
                square, cross = square + tr * tr, cross + f * f.T
            result.append((square, cross))
        return tuple(result)

    carry = tuple(
        (jnp.zeros((1, 1), f32), jnp.zeros((ELEC, ELEC), f32)) for _ in range(slots)
    )

    def announce(carry):
        for o in range(1, groups):
            chol_copies[o - 1].wait_recv()
            carry = terms(other.at[o - 1], carry)

        lane = lax.broadcasted_iota(jnp.int32, (1, LANES), 1)
        energy = jnp.zeros((1, LANES), f32)
        weights = jnp.zeros((1, LANES), f32)
        for w in range(slots):
            square, cross = carry[w]
            two_body = 0.5 * square - 0.5 * jnp.sum(cross, keepdims=True)
            energy = jnp.where(lane == w, one_part[w : w + 1] + two_body / ELEC, energy)
            weights = jnp.where(lane == w, weight_ref[w], weights)
        alive = (lane < count_ref[0]) & (lane < slots)
        sub = lax.broadcasted_iota(jnp.int32, (8, LANES), 0)
        messages[me] = jnp.where(
            sub == 0, energy, jnp.where((sub == 1) & alive, weights, 0.0)
        )

        def tell(d, c):
            j = (me + d) % n
            pltpu.make_async_remote_copy(
                src_ref=messages.at[me], dst_ref=messages.at[me],
                send_sem=sw, recv_sem=rw, device_id=at(j), device_id_type=mesh_ids,
            ).start()
            return c

        lax.fori_loop(1, n, tell, 0)

    leave(1)
    one_rows[...] = one_ref[...].astype(f32)
    theta[ORB:] = jnp.zeros((deep - ORB, slots * LANES), bf16)

    def rows_step(r, c):
        x = padded[:, pl.ds(pl.multiple_of(r * (16 * ELEC), LANES), 16 * LANES)].astype(f32)
        for w in range(slots):
            panel_rows[w, pl.ds(r, 1), :] = x[w : w + 1]
        return c

    turns = ORB // 16
    lax.fori_loop(0, turns, rows_step, 0, unroll=5)
    part_sum = [jnp.zeros((turns, LANES), f32) for w in range(slots)]
    for t in range(15):
        o = one_rows[pl.ds(t, turns, stride=15), :]
        for w in range(slots):
            part_sum[w] = part_sum[w] + panel_rows[w, :turns, t * LANES : (t + 1) * LANES] * o
    one_part = jnp.concatenate(
        [jnp.sum(p, axis=0, keepdims=True) for p in part_sum], axis=0
    )
    one_part = jnp.sum(one_part, axis=1, keepdims=True)
    for w in range(slots):
        for q in range(16):
            theta_rows[pl.ds(w * ORB + q, turns, stride=16), :] = (
                panel_rows[w, :turns, q * ELEC : q * ELEC + LANES]
            )
    for w in range(slots):
        theta[:ORB, w * LANES : (w + 1) * LANES] = (
            theta_rows[w * ORB : (w + 1) * ORB, :].astype(bf16)
        )

    leave(2)
    deliver(0)
    carry = terms(slab, carry)
    most = jnp.zeros((8, LANES), jnp.int32)
    if votes:
        most = counted[...]
        for o in range(1, parts):
            votes[o - 1].wait()
            most = jnp.maximum(most, told[o - 1])
    flag_ref[0] = (jnp.max(most) > room).astype(jnp.int32)
    flag_copy = pltpu.make_async_copy(flag_ref, flag_hbm, out)
    flag_copy.start()
    leave(3)
    deliver(1)
    announce(carry)
    deliver(2)
    deliver(3)

    heard = messages.at[pl.ds(0, n - 1)]
    pltpu.make_async_copy(heard, heard, rw).wait()
    for k in range(STEPS):
        bulk = spread[k].at[pl.ds(0, half - 1)]
        pltpu.make_async_copy(bulk, bulk, r3.at[k]).wait()
        pltpu.make_async_copy(bulk, bulk, s1.at[k]).wait()
        pltpu.make_async_copy(cross[k], cross[k], s2.at[k]).wait()
        pltpu.make_async_copy(bulk, bulk, s3.at[k]).wait()

    for copy in chol_copies:
        copy.wait_send()
    pltpu.make_async_copy(heard, heard, sw).wait()
    flag_copy.wait()


CHUNKS = 1


def finish(
    panel_ref, messages, copy_ref, median_ref, clip_ref,
    energy_hbm, estimate_hbm, fresh_hbm, out_ref,
    energy_ref, estimate_ref, fresh_ref, sems,
):
    n, slots = messages.shape[0], out_ref.shape[0]
    me = lax.axis_index("walk") * lax.axis_size("chol") + lax.axis_index("chol")
    f32 = jnp.float32
    tiles = out_ref.shape[1] // LANES
    copies = []
    for i in range(CHUNKS):
        first, end = tiles * i // CHUNKS, tiles * (i + 1) // CHUNKS
        chunk = pl.ds(first * LANES, (end - first) * LANES)
        copy = pltpu.make_async_copy(
            panel_ref.at[:, chunk], out_ref.at[:, chunk], sems.at[i]
        )
        copy.start()
        copies.append(copy)
    lane = lax.broadcasted_iota(jnp.int32, (1, LANES), 1)
    energy, live = messages[:, 0, :], messages[:, 1, :]
    for w in range(slots):
        energy_ref[w] = jnp.sum(jnp.where(lane == w, messages[me][0:1], 0.0))
    wanted = copy_ref[...].reshape(1, -1)
    slot = lax.broadcasted_iota(jnp.int32, wanted.shape, 1)
    sources = [
        jnp.sum(jnp.where(slot == me * slots + w, wanted, 0), axis=1, keepdims=True)
        for w in range(slots)
    ]
    half_width = jnp.broadcast_to(clip_ref[...].reshape(1, 1), (n, LANES)).astype(f32) / 256.0
    median = jnp.broadcast_to(median_ref[...].reshape(1, 1), (n, LANES))
    clipped = jnp.minimum(jnp.maximum(energy, median - half_width), median + half_width)
    grown = jnp.where(live > 0.0, live * jnp.exp(-tau_step * (clipped - median)), 0.0)
    place = lax.broadcasted_iota(jnp.int32, (n, LANES), 0) * slots
    column = lax.broadcasted_iota(jnp.int32, (n, LANES), 1)
    place = jnp.where(column < slots, place + column, -1)
    weight_sum = jnp.sum(grown, keepdims=True)
    weighted = jnp.sum(grown * clipped, keepdims=True)
    copied = [
        jnp.sum(jnp.where(place == source, grown, 0.0), keepdims=True) for source in sources
    ]
    scale = (n * slots) / weight_sum
    estimate_ref[0] = (weighted / weight_sum)[0, 0]
    for w in range(slots):
        fresh_ref[w] = (copied[w] * scale)[0, 0]
    results = [
        pltpu.make_async_copy(source, target, sems.at[CHUNKS + i])
        for i, (source, target) in enumerate((
            (energy_ref, energy_hbm), (estimate_ref, estimate_hbm), (fresh_ref, fresh_hbm),
        ))
    ]
    for copy in results:
        copy.start()
    for copy in copies + results:
        copy.wait()


def per_device(green, chol_vecs, one_body, weights, counts, copy_list, e_median, clip_bin):
    slots, length = green.shape
    nchol = chol_vecs.shape[0]
    groups = lax.axis_size("chol")
    n = lax.axis_size("walk") * groups
    parts = lax.axis_size("ens")
    tiles = length // LANES
    units = n // 2 * STEPS
    unit = -(-tiles // units)
    width = unit * LANES
    half = n // 2
    deep = -(-ORB // 256) * 256
    wide = max(units * unit, tiles + 1) * LANES
    bf16, f32 = jnp.bfloat16, jnp.float32
    vmem = pl.BlockSpec(memory_space=pltpu.VMEM)
    smem = pl.BlockSpec(memory_space=pltpu.SMEM)
    hbm = pl.BlockSpec(memory_space=pltpu.HBM)
    dma = pltpu.SemaphoreType.DMA

    operands = (
        copy_list, weights, counts,
        green, chol_vecs, one_body.reshape(tiles, LANES),
    )
    def run(room, number, *operands):
        def buffer(rows):
            return [pltpu.VMEM((rows, slots, width), bf16)] * STEPS

        spare = [pltpu.VMEM((1, slots, LANES), bf16)] * STEPS
        return pl.pallas_call(
            functools.partial(body, n, groups, unit, room),
            out_shape=(
                jax.ShapeDtypeStruct((slots, wide), bf16),
                jax.ShapeDtypeStruct((n, 8, LANES), f32),
                jax.ShapeDtypeStruct((1,), jnp.int32),
            ),
            in_specs=[hbm] * 6,
            out_specs=(vmem, vmem, hbm),
            scratch_shapes=[
                    pltpu.VMEM((slots, wide), bf16),
                    pltpu.VMEM((nchol * ELEC, deep), bf16),
                    pltpu.VMEM((groups - 1, nchol * ELEC, deep), bf16),
                    pltpu.VMEM((slots, -(-(ORB // 16) // 8) * 8, 16 * LANES), f32),
                    pltpu.VMEM((slots * ORB, LANES), f32),
                    pltpu.VMEM((deep, slots * LANES), bf16),
                    pltpu.VMEM((nchol * ELEC, deep), f32),
                    pltpu.VMEM((slots, nchol * ELEC, LANES), f32),
                    pltpu.VMEM((tiles, LANES), f32),
                    pltpu.VMEM(chol_vecs.shape, bf16),
                    pltpu.VMEM((tiles, LANES), bf16),
                    pltpu.SMEM(copy_list.shape, jnp.int32),
                    pltpu.SMEM(weights.shape, f32),
                    pltpu.SMEM((1,), jnp.int32),
                    pltpu.SMEM((half * slots,), jnp.int32),
                    pltpu.SMEM((room,), jnp.int32),
                    pltpu.VMEM((8, LANES), jnp.int32),
                    pltpu.VMEM((parts - 1, 8, LANES), jnp.int32),
                    pltpu.SMEM((1,), jnp.int32),
                    dma((STEPS,)), dma((8,)), dma((parts - 1,)), dma((parts - 1,)), dma,
                    *[dma((STEPS,))] * 6,
                    dma((groups - 1,)), dma((groups - 1,)), dma, dma,
                    *buffer(half), *buffer(room // slots),
                    *(buffer(room // slots) if room < half * slots else spare),
                    *buffer(half),
            ],
            compiler_params=pltpu.CompilerParams(
                collective_id=number, has_side_effects=True,
                vmem_limit_bytes=60 * 1024 * 1024,
            ),
        )(*operands)

    def hand_over(panels, messages):
        return pl.pallas_call(
            finish,
            out_shape=(
                jax.ShapeDtypeStruct((slots,), f32),
                jax.ShapeDtypeStruct((1,), f32),
                jax.ShapeDtypeStruct((slots,), f32),
                jax.ShapeDtypeStruct((slots, length), bf16),
            ),
            in_specs=[vmem] * 5,
            out_specs=(hbm,) * 4,
            scratch_shapes=[
                pltpu.SMEM((slots,), f32),
                pltpu.SMEM((1,), f32),
                pltpu.SMEM((slots,), f32),
                dma((CHUNKS + 3,)),
            ],
        )(panels, messages, copy_list, e_median, clip_bin)

    panels, messages, flag = run(min(ROOM, half * slots), 0, *operands)
    return lax.switch(
        flag[0],
        (
            lambda panels, messages, *operands: hand_over(panels, messages),
            lambda panels, messages, *operands: hand_over(
                *run(half * slots, 1, *operands)[:2]
            ),
        ),
        panels, messages, *operands,
    )


def solution(mesh):
    placed = (
        P(("ens", "walk", "chol"), None),
        P("chol", None),
        P(),
        P(("ens", "walk", "chol")),
        P(("ens", "walk", "chol")),
        P("ens"),
        P("ens"),
        P("ens"),
    )
    return jax.shard_map(
        per_device,
        mesh=mesh,
        in_specs=placed,
        out_specs=(
            P(("ens", "walk", "chol")),
            P("ens"),
            P(("ens", "walk", "chol")),
            P(("ens", "walk", "chol"), None),
        ),
        check_vma=False,
    )
```
